32 devices in a mesh: dp: 16 (over z, y, x), tensor: 2 (over core).
Axes of the slice: x: 2, y: 2, z: 4, core: 2. Of those that a mesh axis runs over, the one named last changes fastest.
Arguments:
- text: bfloat16 [15360, 768], P(('dp', 'tensor')), may hold values from -6 to 6
- patches: bfloat16 [192, 145, 1024], P('dp', None, 'tensor'), may hold values from -6 to 6
- segment_ids: int32 [384, 40], P('dp'), may hold values from 0 to 3, never falling along the last dimension, each value on 1 to 20 neighbouring positions
- image_of_row: int32 [384], P('dp'), may hold values from 0 to 11
- gains: bfloat16 [3, 768], replicated, may hold values from 0.25 to 1.75
- shifts: bfloat16 [3, 768], replicated, may hold values from -1.5 to 1.5
- self_qkv: bfloat16 [768, 3, 768], P(None, None, 'tensor'), may hold values from -0.21875 to 0.21875
- in_bias: bfloat16 [4, 768], P(None, 'tensor'), may hold values from -1 to 1
- self_out: bfloat16 [768, 768], P('tensor'), may hold values from -0.625 to 0.625
- cross_q: bfloat16 [768, 768], P(None, 'tensor'), may hold values from -0.21875 to 0.21875
- cross_kv: bfloat16 [1024, 2, 768], P(None, None, 'tensor'), may hold values from -0.1875 to 0.1875
- cross_out: bfloat16 [768, 768], P('tensor'), may hold values from -1.75 to 1.75
- ffn_in: bfloat16 [768, 3072], P(None, 'tensor'), may hold values from -0.21875 to 0.21875
- ffn_in_bias: bfloat16 [3072], P('tensor'), may hold values from -2.5 to 2.5
- ffn_out: bfloat16 [3072, 768], P('tensor'), may hold values from -0.109375 to 0.109375
- out_bias: bfloat16 [3, 768], replicated, may hold values from -1.5 to 1.5
- cotangent: bfloat16 [15360, 768], P(('dp', 'tensor')), may hold values from -6 to 6
Outputs:
- layer_out: float32 [15360, 768], P(('dp', 'tensor'))
- text_grad: float32 [15360, 768], P(('dp', 'tensor'))
- patch_grad: float32 [192, 145, 1024], P('dp', None, 'tensor')
- gains_grad: float32 [3, 768], replicated
- shifts_grad: float32 [3, 768], replicated
- self_qkv_grad: float32 [768, 3, 768], P(None, None, 'tensor')
- in_bias_grad: float32 [4, 768], P(None, 'tensor')
- self_out_grad: float32 [768, 768], P('tensor')
- cross_q_grad: float32 [768, 768], P(None, 'tensor')
- cross_kv_grad: float32 [1024, 2, 768], P(None, None, 'tensor')
- cross_out_grad: float32 [768, 768], P('tensor')
- ffn_in_grad: float32 [768, 3072], P(None, 'tensor')
- ffn_in_bias_grad: float32 [3072], P('tensor')
- ffn_out_grad: float32 [3072, 768], P('tensor')
- out_bias_grad: float32 [3, 768], replicated
The draws below stay inside these ranges and needn't reach their ends.
All inputs are finite; a program needn't handle non-finite values.
Results may differ from the reference program's by a relative error of at most 0.018.
Values may be sent and summed in bfloat16 or wider, within the bound.
No kernel may reach another device: no remote copies, remote signals or barrier semaphores. Data moves between devices by JAX's collectives and lax.ppermute only.
A program may use at most 192 MiB of HBM per device.

```python
import math
import jax
import jax.numpy as jnp
import numpy as np
from jax import lax

D = 768
HEADS = 12
HEAD = 64
FF = 3072
DV = 1024
PATCHES = 145
LEN = 40
ROWS_DEV = 24
IMG_DEV = 12
ROWS = 384
IMAGES = 192
TOKENS = 15360
N_DP = 16


def with_ends(array, own_key, smallest, largest):
    longest = array.shape.index(max(array.shape))
    spots = []
    for shift in (0, 1):
        where = [jax.random.randint(jax.random.fold_in(own_key, axis), (), 0, length) for axis, length in enumerate(array.shape)]
        where[longest] = (where[longest] + shift) % array.shape[longest]
        spots.append(tuple(where))
    return array.at[spots[0]].set(smallest).at[spots[1]].set(largest)


def raised(values, key, source, target, shards_of, factor):
    def block_of(dim):
        return (jnp.arange(values.shape[dim]) // (values.shape[dim] // shards_of)).reshape((-1,) + (1,) * (values.ndim - 1 - dim))

    near = jax.random.permutation(key, shards_of)[block_of(target)]
    second = (block_of(target) + shards_of // 2) % shards_of
    return jnp.where((block_of(source) == near) | (block_of(source) == second), factor * values, values)


def shard_levels(stream_key, shape, cuts, low, largest):
    def one(axis_at, parts):
        draws = jax.random.uniform(jax.random.fold_in(jax.random.fold_in(stream_key, 6), axis_at), (parts,), jnp.float32, low / len(cuts), largest / len(cuts))
        return jnp.repeat(jnp.exp(draws), shape[axis_at] // parts).reshape((-1,) + (1,) * (len(shape) - axis_at - 1))

    loudness = one(*cuts[0])
    for cut in cuts[1:]:
        loudness = loudness * one(*cut)
    return loudness


def split_up(number_of, total, bound, skew):
    portions = [(1 << 20) // math.isqrt(standing ** skew) + 1 for standing in range(2, number_of + 1)]
    spare, holding = total - bound - (number_of - 1), [1] * (number_of - 1)
    while spare > 0:
        free = [i for i in range(number_of - 1) if holding[i] < bound]
        mass, remaining = sum([portions[i] for i in free]), spare
        for i in free:
            more = min(bound - holding[i], max(1, remaining * portions[i] // mass), spare)
            holding[i] = holding[i] + more
            spare = spare - more
    return np.array([bound] + holding)


def ragged(stream_key, count, total, bound, lean):
    if count == 2:
        one = jax.random.randint(stream_key, (), max(1, total - bound), min(bound, total - 1) + 1)
        return jnp.stack([one, total - one])
    sizes = jnp.asarray(split_up(count, total, bound, lean), jnp.int32)
    twos = (count - 1) // 2
    giver, receiver = sizes[1:1 + 2 * twos:2], sizes[2:2 + 2 * twos:2]
    slack = jnp.minimum(giver - 1, bound - receiver)
    shifted = jax.random.randint(jax.random.fold_in(stream_key, 1), (twos,), 0, 1 << 20) % (slack + 1)
    sizes = sizes.at[1:1 + 2 * twos:2].set(giver - shifted).at[2:2 + 2 * twos:2].set(receiver + shifted)
    return sizes[jax.random.permutation(jax.random.fold_in(stream_key, 2), count)]


def scatter_about(own_key, extent, scale, bound, split=(), held_as=jnp.bfloat16):
    loudness = shard_levels(own_key, extent, split, -0.22, 0.18) if split else 1.0
    values = jax.random.normal(own_key, extent, jnp.float32) * scale * loudness
    return jnp.minimum(jnp.maximum(values, -bound), bound).astype(held_as)


def noise_with(own_key, dims, width, bound, cuts, heavy, held_as=jnp.bfloat16):
    values = width * jax.random.normal(own_key, dims, jnp.float32)
    if cuts:
        values = values * shard_levels(own_key, dims, cuts, -0.22, 0.18)
    return jnp.clip(raised(values, jax.random.fold_in(own_key, 3), *heavy), -bound, bound).astype(held_as)


def setup_inputs(seed: int = 0) -> dict:
    keys = jax.random.split(jax.random.key(seed), 18)
    text = noise_with(keys[0], (TOKENS, D), 1.0, 6.0, ((0, 32),), (0, 1, 32, 2.75))
    patches = scatter_about(keys[1], (IMAGES, PATCHES, DV), 1.0, 6.0, ((0, 16), (2, 2)))
    segment_ids = jax.vmap(lambda own: jnp.searchsorted(jnp.cumsum(ragged(own, 4, LEN, LEN // 2, 1)), jnp.arange(LEN), side="right"))(jax.random.split(keys[2], ROWS)).reshape((ROWS, LEN)).astype(jnp.int32)
    image_of_row = with_ends(jax.random.randint(keys[3], (ROWS,), 0, IMG_DEV), jax.random.fold_in(keys[3], 1), 0, IMG_DEV - 1).astype(jnp.int32)
    gains = jnp.clip(1.0 + 0.15 * jax.random.normal(keys[4], (3, D), jnp.float32), 0.25, 1.75).astype(jnp.bfloat16)
    shifts = scatter_about(keys[5], (3, D), 0.3, 1.5)
    self_qkv = scatter_about(keys[6], (D, 3, D), D ** -0.5, 0.21875, ((2, 2),))
    in_bias = scatter_about(keys[7], (4, D), 0.2, 1.0, ((1, 2),))
    self_out = scatter_about(keys[8], (D, D), (D // 8) ** -0.5, 0.625, ((0, 2),))
    cross_q = scatter_about(keys[9], (D, D), D ** -0.5, 0.21875, ((1, 2),))
    cross_kv = scatter_about(keys[10], (DV, 2, D), DV ** -0.5, 0.1875, ((2, 2),))
    cross_out = scatter_about(keys[11], (D, D), (D // 64) ** -0.5, 1.75, ((0, 2),))
    ffn_in = scatter_about(keys[12], (D, FF), D ** -0.5, 0.21875, ((1, 2),))
    ffn_in_bias = scatter_about(keys[13], (FF,), 0.5, 2.5, ((0, 2),))
    ffn_out = scatter_about(keys[14], (FF, D), FF ** -0.5, 0.109375, ((0, 2),))
    out_bias = scatter_about(keys[15], (3, D), 0.3, 1.5)
    cotangent = noise_with(keys[16], (TOKENS, D), 1.0, 6.0, ((0, 32),), (0, 1, 32, 2.75))
    return {"text": text, "patches": patches, "segment_ids": segment_ids, "image_of_row": image_of_row, "gains": gains, "shifts": shifts, "self_qkv": self_qkv, "in_bias": in_bias, "self_out": self_out, "cross_q": cross_q, "cross_kv": cross_kv, "cross_out": cross_out, "ffn_in": ffn_in, "ffn_in_bias": ffn_in_bias, "ffn_out": ffn_out, "out_bias": out_bias, "cotangent": cotangent}


@jax.custom_vjp
def low(v):
    return lax.optimization_barrier(v.astype(jnp.bfloat16)).astype(jnp.float32)

@jax.custom_vjp
def low_back(v):
    return v

def low_keep(v):
    return (low(v), None)

def low_pass(kept, grad):
    return (grad,)

def back_keep(v):
    return (v, None)

def back_low(kept, grad):
    return (low(grad),)
low.defvjp(low_keep, low_pass)
low_back.defvjp(back_keep, back_low)
EPSILON = 1e-06
SCORE_SCALE = 0.125
NEGATIVE = -1000000000.0
PRECISE = lax.Precision.HIGHEST

def norm_rows(values, gain_row, shift_row):
    centre = values - lax.optimization_barrier(jnp.mean(values, axis=-1, keepdims=True))
    spread = lax.optimization_barrier(jnp.mean(centre * centre, axis=-1, keepdims=True))
    return centre * lax.rsqrt(spread + EPSILON) * gain_row + shift_row

def block_forward(params, pieces):
    gains, shifts, self_qkv, in_bias, self_out, cross_q, cross_kv, cross_out, ffn_in, ffn_in_bias, ffn_out, out_bias = params
    rows_text, rows_patch, rows_segment, rows_image = pieces
    quad = (ROWS_DEV, LEN, HEADS, HEAD)
    patch_quad = (ROWS_DEV, PATCHES, HEADS, HEAD)
    resid = rows_text
    normed = low(norm_rows(resid, gains[0], shifts[0]))
    project = jnp.einsum('td,dke->tke', normed, self_qkv, precision=PRECISE)
    queries = low(low_back(project[:, 0] + in_bias[0])).reshape(quad)
    keys_self = low(low_back(project[:, 1])).reshape(quad)
    values_self = low(low_back(project[:, 2] + in_bias[1])).reshape(quad)
    same = (rows_segment[:, :, None] == rows_segment[:, None, :])[:, None]
    scores = low_back(jnp.einsum('rqhe,rkhe->rhqk', queries, keys_self, precision=PRECISE) * SCORE_SCALE)
    probs = low(jax.nn.softmax(jnp.where(same, scores, NEGATIVE), axis=-1))
    attended = low(low_back(jnp.einsum('rhqk,rkhe->rqhe', probs, values_self, precision=PRECISE).reshape(-1, D)))
    resid = resid + low_back(jnp.dot(attended, self_out, precision=PRECISE)) + out_bias[0]
    normed = low(norm_rows(resid, gains[1], shifts[1]))
    cross_queries = low(low_back(jnp.dot(normed, cross_q, precision=PRECISE) + in_bias[2])).reshape(quad)
    patch_proj = jnp.einsum('ipf,fje->ipje', rows_patch, cross_kv, precision=PRECISE)
    patch_keys = low(low_back(patch_proj[:, :, 0]))
    patch_values = low(low_back(patch_proj[:, :, 1] + in_bias[3]))
    pick = (rows_image[:, None] == jnp.arange(IMG_DEV)[None, :]).astype(jnp.float32)
    row_keys = jnp.einsum('ri,ipe->rpe', pick, patch_keys, precision=PRECISE).reshape(patch_quad)
    row_values = jnp.einsum('ri,ipe->rpe', pick, patch_values, precision=PRECISE).reshape(patch_quad)
    scores = low_back(jnp.einsum('rqhe,rphe->rhqp', cross_queries, row_keys, precision=PRECISE) * SCORE_SCALE)
    probs = low(jax.nn.softmax(scores, axis=-1))
    attended = low(low_back(jnp.einsum('rhqp,rphe->rqhe', probs, row_values, precision=PRECISE).reshape(-1, D)))
    resid = resid + low_back(jnp.dot(attended, cross_out, precision=PRECISE)) + out_bias[1]
    normed = low(norm_rows(resid, gains[2], shifts[2]))
    inner = low_back(jnp.dot(normed, ffn_in, precision=PRECISE) + ffn_in_bias)
    hidden = low(jax.nn.gelu(inner, approximate=False))
    return resid + low_back(jnp.dot(hidden, ffn_out, precision=PRECISE)) + out_bias[2]

def layer(text_in, patch_in, params, segment_ids, image_of_row):
    pieces = (text_in.reshape(N_DP, ROWS_DEV * LEN, D), patch_in.reshape(N_DP, IMG_DEV, PATCHES, DV), segment_ids.reshape(N_DP, ROWS_DEV, LEN), image_of_row.reshape(N_DP, ROWS_DEV))
    stepper = jax.checkpoint(block_forward)
    outputs = lax.map(lambda piece: stepper(params, piece), pieces)
    return outputs.reshape(-1, D)

def reference(text, patches, segment_ids, image_of_row, gains, shifts, self_qkv, in_bias, self_out, cross_q, cross_kv, cross_out, ffn_in, ffn_in_bias, ffn_out, out_bias, cotangent):
    params = tuple((member.astype(jnp.float32) for member in (gains, shifts, self_qkv, in_bias, self_out, cross_q, cross_kv, cross_out, ffn_in, ffn_in_bias, ffn_out, out_bias)))

    def wrapped(text_in, patch_in, weights):
        return layer(text_in, patch_in, weights, segment_ids, image_of_row)
    result, pullback = jax.vjp(wrapped, text.astype(jnp.float32), patches.astype(jnp.float32), params)
    text_grad, patch_grad, grads = pullback(cotangent.astype(jnp.float32))
    return (result, text_grad, patch_grad, grads[0], grads[1], grads[2], grads[3], grads[4], grads[5], grads[6], grads[7], grads[8], grads[9], grads[10], grads[11])
```

```python
import functools

import jax
import jax.numpy as jnp
from jax import lax
from jax.experimental import pallas as pl
from jax.experimental.pallas import tpu as pltpu
from jax.sharding import PartitionSpec as P

HEAD = 64
EPSILON = 1e-06
SCALE = 0.125
NEGATIVE = -1000000000.0
F32 = jnp.float32
BF16 = jnp.bfloat16
VMEM_BYTES = 60 * 1024 * 1024


def dot_nn(a, b):
    return lax.dot_general(a, b, (((1,), (0,)), ((), ())), preferred_element_type=F32)


def dot_nt(a, b):
    return lax.dot_general(a, b, (((1,), (1,)), ((), ())), preferred_element_type=F32)


def dot_tn(a, b):
    return lax.dot_general(a, b, (((0,), (0,)), ((), ())), preferred_element_type=F32)


def norm_parts(v):
    centre = v - jnp.mean(v, axis=-1, keepdims=True)
    spread = jnp.mean(centre * centre, axis=-1, keepdims=True)
    r = lax.rsqrt(spread + EPSILON)
    return centre * r, r


def norm_back(dn, y, r, gain):
    w = dn * gain
    return r * (w - jnp.mean(w, axis=-1, keepdims=True) - y * jnp.mean(w * y, axis=-1, keepdims=True))


def spread_heads(row, heads):
    column = lax.broadcasted_iota(jnp.int32, row.shape, 1) // HEAD
    return jnp.concatenate(
        [jnp.where(column == h, row, 0.0) for h in range(heads)], axis=0
    ).astype(BF16)


def join_heads(wide, length, heads):
    column = lax.broadcasted_iota(jnp.int32, (length, heads * HEAD), 1) // HEAD
    out = wide[0:length]
    for h in range(1, heads):
        out = jnp.where(column == h, wide[h * length : (h + 1) * length], out)
    return out


def softmax_columns(st):
    top = jnp.max(st, axis=0, keepdims=True)
    e = jnp.exp(st - top)
    return e / jnp.sum(e, axis=0, keepdims=True)


def self_fwd_kernel(rows, length, heads, half, xo, xp, gains, shifts, w, bias, wo, segk, segq,
                    n1, q, k, v, p, a, part):
    i = pl.program_id(0)
    x = jnp.where(i < half, xo[...].astype(F32), xp[...].astype(F32))
    y, _ = norm_parts(x)
    n = (y * gains[0:1, :].astype(F32) + shifts[0:1, :].astype(F32)).astype(BF16)
    n1[...] = n
    b = bias[...].astype(F32)
    qv = (dot_nn(n, w[0]) + b[0:1]).astype(BF16)
    kv = dot_nn(n, w[1]).astype(BF16)
    vv = (dot_nn(n, w[2]) + b[1:2]).astype(BF16)
    q[...] = qv
    k[...] = kv
    v[...] = vv
    qf, kf, vf = qv.astype(F32), kv.astype(F32), vv.astype(F32)
    outs = []
    for r in range(rows):
        at = slice(r * length, (r + 1) * length)
        kr = kf[at].astype(BF16)
        vr = vf[at].astype(BF16)
        st = dot_nt(kr, spread_heads(qf[at], heads)) * SCALE
        st = jnp.where(segk[r] == segq[r], st, NEGATIVE)
        pr = softmax_columns(st).astype(BF16)
        p[r] = pr
        outs.append(join_heads(dot_tn(pr, vr), length, heads))
    av = jnp.concatenate(outs, axis=0).astype(BF16)
    a[...] = av
    part[...] = dot_nn(av, wo[...]).astype(BF16)


def project_kernel(place, po, pp, w0, w1, bias, kv):
    x = dot_nn(po[0], w0[...]) + dot_nn(pp[0], w1[...])
    kv[0] = (x + bias[...]).astype(BF16)


def cross_fwd_kernel(rows, length, heads, half, pick, xo, xp, part, recv, gains, shifts, bias, out_bias,
                     wq, kv, wo, h1, n2, c2, p, a, part2):
    i = pl.program_id(0)
    x = jnp.where(i < half, xo[...].astype(F32), xp[...].astype(F32))
    h = x + (part[...].astype(F32) + recv[...].astype(F32)) + out_bias[0:1, :].astype(F32)
    h1[...] = h
    y, _ = norm_parts(h)
    n = (y * gains[1:2, :].astype(F32) + shifts[1:2, :].astype(F32)).astype(BF16)
    n2[...] = n
    cv = (dot_nn(n, wq[...]) + bias[2:3, :].astype(F32)).astype(BF16)
    c2[...] = cv
    cf = cv.astype(F32)
    width = heads * HEAD
    outs = []
    for r in range(rows):
        at = slice(r * length, (r + 1) * length)
        im = pick[i * rows + r]
        kr = kv[im, :, 0:width]
        vr = kv[im, :, width : 2 * width]
        st = dot_nt(kr, spread_heads(cf[at], heads)) * SCALE
        pr = softmax_columns(st).astype(BF16)
        p[r] = pr
        outs.append(join_heads(dot_tn(pr, vr), length, heads))
    av = jnp.concatenate(outs, axis=0).astype(BF16)
    a[...] = av
    part2[...] = dot_nn(av, wo[...]).astype(BF16)


def ffn_kernel(half, chunk, h1, part, recv, eo, ep, gains, shifts, out_bias, w_in, b_in, w_out,
               h2, n3, m3, du3, e3, part_own, part_par, pdn, b_grad):
    i = pl.program_id(0)
    h = h1[...] + (part[...].astype(F32) + recv[...].astype(F32)) + out_bias[1:2, :].astype(F32)
    h2[...] = h
    y, _ = norm_parts(h)
    n = (y * gains[2:3, :].astype(F32) + shifts[2:3, :].astype(F32)).astype(BF16)
    n3[...] = n
    e = jnp.where(i < half, eo[...].astype(F32), ep[...].astype(F32)).astype(BF16)
    e3[...] = e

    @pl.when(i == 0)
    def _():
        b_grad[...] = jnp.zeros_like(b_grad)

    out_sum = None
    back_sum = None
    for c in range(w_in.shape[1] // chunk):
        at = slice(c * chunk, (c + 1) * chunk)
        u = dot_nn(n, w_in[:, at]) + b_in[:, at].astype(F32)
        cdf = 0.5 * (1.0 + lax.erf(u * 0.7071067811865476))
        m = (u * cdf).astype(BF16)
        m3[:, at] = m
        slope = cdf + u * (jnp.exp(-0.5 * u * u) * 0.3989422804014327)
        d = (dot_nt(e, w_out[at, :]) * slope).astype(BF16)
        du3[:, at] = d
        b_grad[:, at] += jnp.sum(d.astype(F32), axis=0, keepdims=True)
        o = dot_nn(m, w_out[at, :])
        g = dot_nt(d, w_in[:, at])
        out_sum = o if out_sum is None else out_sum + o
        back_sum = g if back_sum is None else back_sum + g
    pdn[...] = back_sum.astype(BF16)

    @pl.when(i < half)
    def _():
        part_own[...] = out_sum.astype(BF16)

    @pl.when(i >= half)
    def _():
        part_par[...] = out_sum.astype(BF16)


def cross_bwd_kernel(rows, length, heads, half, pick, h2, part, recv, eo, ep, gains, wo, c2, p, kv, wq,
                     dh2, e2, dc2, dkv, pdn, sums, dk_acc, dv_acc):
    i = pl.program_id(0)
    width = heads * HEAD

    @pl.when(i == 0)
    def _():
        sums[...] = jnp.zeros_like(sums)
        dk_acc[...] = jnp.zeros_like(dk_acc)
        dv_acc[...] = jnp.zeros_like(dv_acc)

    dn = part[...].astype(F32) + recv[...].astype(F32)
    y, rs = norm_parts(h2[...])
    g3 = jnp.where(i < half, eo[...].astype(F32), ep[...].astype(F32))
    d = g3 + norm_back(dn, y, rs, gains[2:3, :].astype(F32))
    dh2[...] = d
    e = d.astype(BF16)
    e2[...] = e

    @pl.when(i < half)
    def _():
        sums[0:1, :] += jnp.sum(dn * y, axis=0, keepdims=True)
        sums[1:2, :] += jnp.sum(dn, axis=0, keepdims=True)
        sums[2:3, :] += jnp.sum(d, axis=0, keepdims=True)
        sums[3:4, :] += jnp.sum(g3, axis=0, keepdims=True)

    da = dot_nt(e, wo[...]).astype(BF16).astype(F32)
    cf = c2[...].astype(F32)
    outs = []
    for r in range(rows):
        at = slice(r * length, (r + 1) * length)
        im = pick[i * rows + r]
        kr = kv[im, :, 0:width]
        vr = kv[im, :, width : 2 * width]
        pr = p[r]
        wide_o = spread_heads(da[at], heads)
        dpt = dot_nt(vr, wide_o)
        dv_acc[im] += dot_nn(pr, wide_o)
        pf = pr.astype(F32)
        ds = (pf * (dpt - jnp.sum(pf * dpt, axis=0, keepdims=True))).astype(BF16)
        outs.append(join_heads(dot_tn(ds, kr), length, heads))
        dk_acc[im] += dot_nn(ds, spread_heads(cf[at], heads)) * SCALE
    dc = (jnp.concatenate(outs, axis=0) * SCALE).astype(BF16)
    dc2[...] = dc
    pdn[...] = dot_nt(dc, wq[...]).astype(BF16)

    @pl.when(i == pl.num_programs(0) - 1)
    def _():
        dkv[:, :, 0:width] = dk_acc[...].astype(BF16)
        dkv[:, :, width : 2 * width] = dv_acc[...].astype(BF16)


def self_bwd_kernel(rows, length, heads, half, h1, dh2, part, recv, gains, wo, q, k, v, p, w,
                    dh1, e1, dq, dk, dv, part_own, part_par, sums, sums_in):
    i = pl.program_id(0)

    @pl.when(i == 0)
    def _():
        sums[...] = jnp.zeros_like(sums)
        sums_in[...] = jnp.zeros_like(sums_in)

    dn = part[...].astype(F32) + recv[...].astype(F32)
    y, rs = norm_parts(h1[...])
    d = dh2[...] + norm_back(dn, y, rs, gains[1:2, :].astype(F32))
    e = d.astype(BF16)
    e1[...] = e

    @pl.when(i < half)
    def _():
        dh1[...] = d
        sums[0:1, :] += jnp.sum(dn * y, axis=0, keepdims=True)
        sums[1:2, :] += jnp.sum(dn, axis=0, keepdims=True)
        sums[2:3, :] += jnp.sum(d, axis=0, keepdims=True)

    da = dot_nt(e, wo[...]).astype(BF16).astype(F32)
    qf, kf, vf = q[...].astype(F32), k[...].astype(F32), v[...].astype(F32)
    oq, ok, ov = [], [], []
    for r in range(rows):
        at = slice(r * length, (r + 1) * length)
        kr = kf[at].astype(BF16)
        vr = vf[at].astype(BF16)
        pr = p[r]
        wide_o = spread_heads(da[at], heads)
        dpt = dot_nt(vr, wide_o)
        ov.append(dot_nn(pr, wide_o))
        pf = pr.astype(F32)
        ds = (pf * (dpt - jnp.sum(pf * dpt, axis=0, keepdims=True))).astype(BF16)
        oq.append(join_heads(dot_tn(ds, kr), length, heads))
        ok.append(dot_nn(ds, spread_heads(qf[at], heads)))
    dqv = (jnp.concatenate(oq, axis=0) * SCALE).astype(BF16)
    dkv = (jnp.concatenate(ok, axis=0) * SCALE).astype(BF16)
    dvv = jnp.concatenate(ov, axis=0).astype(BF16)
    dq[...] = dqv
    dk[...] = dkv
    dv[...] = dvv
    sums_in[0:1, :] += jnp.sum(dqv.astype(F32), axis=0, keepdims=True)
    sums_in[1:2, :] += jnp.sum(dvv.astype(F32), axis=0, keepdims=True)
    back = (dot_nt(dqv, w[0]) + dot_nt(dkv, w[1]) + dot_nt(dvv, w[2])).astype(BF16)

    @pl.when(i < half)
    def _():
        part_own[...] = back

    @pl.when(i >= half)
    def _():
        part_par[...] = back


def text_bwd_kernel(x, dh1, part, recv, gains, out, sums):
    i = pl.program_id(0)

    @pl.when(i == 0)
    def _():
        sums[...] = jnp.zeros_like(sums)

    dn = part[...].astype(F32) + recv[...].astype(F32)
    y, rs = norm_parts(x[...].astype(F32))
    out[...] = dh1[...] + norm_back(dn, y, rs, gains[0:1, :].astype(F32))
    sums[0:1, :] += jnp.sum(dn * y, axis=0, keepdims=True)
    sums[1:2, :] += jnp.sum(dn, axis=0, keepdims=True)


def whole(shape):
    zeros = (0,) * len(shape)
    return pl.BlockSpec(shape, lambda i, *_: zeros)


def call(kernel, name, grid, ins, outs, args, scratch=(), prefetch=0, flops=0, exps=0):
    moved = sum(a.size * a.dtype.itemsize for a in args) + sum(
        functools.reduce(lambda u, v: u * v, s.shape, 1) * s.dtype.itemsize for s, _ in outs
    )
    return pl.pallas_call(
        kernel,
        out_shape=[s for s, _ in outs],
        grid_spec=pltpu.PrefetchScalarGridSpec(
            num_scalar_prefetch=prefetch,
            grid=grid,
            in_specs=list(ins),
            out_specs=[b for _, b in outs],
            scratch_shapes=list(scratch),
        ),
        compiler_params=pltpu.CompilerParams(vmem_limit_bytes=VMEM_BYTES),
        cost_estimate=pl.CostEstimate(flops=flops, transcendentals=exps, bytes_accessed=moved),
        name=name,
    )(*args)


def local(n_dp, orders, text, patches, segment_ids, image_of_row, gains, shifts, self_qkv, in_bias, self_out,
          cross_q, cross_kv, cross_out, ffn_in, ffn_in_bias, ffn_out, out_bias, cotangent):
    core = lax.axis_index("tensor")
    dp = lax.axis_index("dp")
    own, width = text.shape
    tokens = 2 * own
    rows, length = segment_ids.shape
    local_width = self_out.shape[0]
    heads = local_width // HEAD
    images, spots, half_dv = patches.shape
    hidden = ffn_in.shape[1]
    block_rows = 6 if (rows // 2) % 6 == 0 else 1
    block = block_rows * length
    steps = tokens // block
    half = steps // 2
    sd = jax.ShapeDtypeStruct

    swap = lambda v: lax.ppermute(v, "tensor", [(0, 1), (1, 0)])
    text_par = swap(text)
    cot_par = swap(cotangent)
    patches_par = swap(patches)

    w3 = jnp.transpose(self_qkv, (1, 0, 2))
    wkv = cross_kv.reshape(cross_kv.shape[0], 2 * local_width)
    flip = lambda v: jnp.where(core == 0, v, jnp.roll(v, rows // 2, axis=0))
    seg = flip(segment_ids)
    pick = flip(image_of_row)
    segk = seg[:, :, None]
    segq = jnp.tile(seg, (1, heads))[:, None, :]

    tok = lambda n: pl.BlockSpec((block, n), lambda i, *_: (i, 0))
    tok_other = lambda n: pl.BlockSpec((block, n), lambda i, *_: ((i + half) % steps, 0))
    tok_own = lambda n: pl.BlockSpec((block, n), lambda i, *_: (jnp.minimum(i, half - 1), 0))
    tok_par = lambda n: pl.BlockSpec((block, n), lambda i, *_: (jnp.maximum(i - half, 0), 0))
    row3 = lambda a, b: pl.BlockSpec((block_rows, a, b), lambda i, *_: (i, 0, 0))
    act = lambda n, dt=BF16: (sd((tokens, n), dt), tok(n))
    ql = heads * length
    sizes = (block_rows, length, heads, half)

    n1, q, k, v, p1, a1, part1 = call(
        functools.partial(self_fwd_kernel, *sizes), "self_fwd", (steps,),
        [tok_own(width), tok_par(width), whole(gains.shape), whole(shifts.shape), whole(w3.shape),
         whole(in_bias.shape), whole(self_out.shape), row3(length, 1), row3(1, ql)],
        [act(width), act(local_width), act(local_width), act(local_width),
         (sd((rows, length, ql), BF16), row3(length, ql)), act(local_width), act(width)],
        (text, text_par, gains, shifts, w3, in_bias, self_out, segk, segq),
        flops=2 * tokens * width * 4 * local_width, exps=rows * length * ql)
    recv1 = swap(part1)

    kv_bias = jnp.concatenate([jnp.zeros((local_width,), F32), in_bias[3].astype(F32)])[None, :]
    place = jnp.full((1,), core, jnp.int32)
    (kv,) = call(
        project_kernel, "project", (images,),
        [pl.BlockSpec((1, spots, half_dv), lambda i, *_: (i, 0, 0)),
         pl.BlockSpec((1, spots, half_dv), lambda i, *_: (i, 0, 0)),
         pl.BlockSpec((half_dv, 2 * local_width), lambda i, c: (c[0], 0)),
         pl.BlockSpec((half_dv, 2 * local_width), lambda i, c: (1 - c[0], 0)),
         whole(kv_bias.shape)],
        [(sd((images, spots, 2 * local_width), BF16),
          pl.BlockSpec((1, spots, 2 * local_width), lambda i, *_: (i, 0, 0)))],
        (place, patches, patches_par, wkv, wkv, kv_bias), prefetch=1,
        flops=4 * images * spots * 2 * half_dv * local_width)

    h1, n2, c2, p2, a2, part2 = call(
        functools.partial(cross_fwd_kernel, *sizes), "cross_fwd", (steps,),
        [tok_own(width), tok_par(width), tok(width), tok_other(width), whole(gains.shape), whole(shifts.shape),
         whole(in_bias.shape), whole(out_bias.shape), whole(cross_q.shape), whole(kv.shape), whole(cross_out.shape)],
        [act(width, F32), act(width), act(local_width), (sd((rows, spots, ql), BF16), row3(spots, ql)),
         act(local_width), act(width)],
        (pick, text, text_par, part1, recv1, gains, shifts, in_bias, out_bias, cross_q, kv, cross_out), prefetch=1,
        flops=2 * tokens * width * 2 * local_width + 4 * rows * ql * spots * local_width, exps=rows * ql * spots)
    recv2 = swap(part2)

    own_spec = lambda n: (sd((own, n), BF16), tok_own(n))
    par_spec = lambda n: (sd((own, n), BF16), tok_par(n))
    b_in = ffn_in_bias[None, :]
    h2, n3, m3, du3, e3, part3_own, part3_par, pdn3, ffn_in_bias_grad = call(
        functools.partial(ffn_kernel, half, 512 if hidden % 512 == 0 else hidden), "ffn", (steps,),
        [tok(width), tok(width), tok_other(width), tok_own(width), tok_par(width), whole(gains.shape),
         whole(shifts.shape), whole(out_bias.shape), whole(ffn_in.shape), whole(b_in.shape), whole(ffn_out.shape)],
        [act(width, F32), act(width), act(hidden), act(hidden), act(width), own_spec(width), par_spec(width),
         act(width), (sd((1, hidden), F32), whole((1, hidden)))],
        (h1, part2, recv2, cotangent, cot_par, gains, shifts, out_bias, ffn_in, b_in, ffn_out),
        flops=8 * tokens * width * hidden, exps=2 * tokens * hidden)
    recv3 = swap(pdn3)
    recv_out = swap(part3_par)
    layer_out = h2[:own] + (part3_own.astype(F32) + recv_out.astype(F32)) + out_bias[2].astype(F32)

    g_ffn_out = dot_tn(m3, e3).astype(BF16)
    g_ffn_in = dot_tn(n3, du3).astype(BF16)

    dh2, e2, dc2, dkv, pdn2, sums2 = call(
        functools.partial(cross_bwd_kernel, *sizes), "cross_bwd", (steps,),
        [tok(width), tok(width), tok_other(width), tok_own(width), tok_par(width), whole(gains.shape),
         whole(cross_out.shape), tok(local_width), row3(spots, ql), whole(kv.shape), whole(cross_q.shape)],
        [act(width, F32), act(width), act(local_width), (sd(kv.shape, BF16), whole(kv.shape)), act(width),
         (sd((8, width), F32), whole((8, width)))],
        (pick, h2, pdn3, recv3, cotangent, cot_par, gains, cross_out, c2, p2, kv, cross_q), prefetch=1,
        scratch=[pltpu.VMEM((images, spots, local_width), F32)] * 2,
        flops=2 * tokens * width * 2 * local_width + 8 * rows * ql * spots * local_width)
    recv_dn2 = swap(pdn2)

    g_cross_out = dot_tn(a2, e2).astype(BF16)
    g_cross_q = dot_tn(n2, dc2).astype(BF16)
    contract_images = lambda a: lax.dot_general(
        a, dkv, (((0, 1), (0, 1)), ((), ())), preferred_element_type=F32).astype(BF16)
    g_kv_own = contract_images(patches)
    g_kv_par = contract_images(patches_par)
    w_own = lax.dynamic_slice_in_dim(wkv, core * half_dv, half_dv, axis=0)
    w_par = lax.dynamic_slice_in_dim(wkv, (1 - core) * half_dv, half_dv, axis=0)
    terms = lambda w: lax.dot_general(dkv, w, (((2,), (1,)), ((), ())), preferred_element_type=F32)
    patch_grad = terms(w_own) + swap(terms(w_par).astype(BF16)).astype(F32)
    cross_q_bias = jnp.sum(dc2.astype(F32), axis=0)
    cross_v_bias = jnp.sum(dkv[:, :, local_width:].astype(F32), axis=(0, 1))

    dh1, e1, dq, dk, dv, part1_own, part1_par, sums1, sums_in = call(
        functools.partial(self_bwd_kernel, *sizes), "self_bwd", (steps,),
        [tok(width), tok(width), tok(width), tok_other(width), whole(gains.shape), whole(self_out.shape),
         tok(local_width), tok(local_width), tok(local_width), row3(length, ql), whole(w3.shape)],
        [(sd((own, width), F32), tok_own(width)), act(width), act(local_width), act(local_width), act(local_width),
         own_spec(width), par_spec(width), (sd((8, width), F32), whole((8, width))),
         (sd((8, local_width), F32), whole((8, local_width)))],
        (h1, dh2, pdn2, recv_dn2, gains, self_out, q, k, v, p1, w3),
        flops=2 * tokens * width * 4 * local_width)
    recv_dn1 = swap(part1_par)

    g_self_out = dot_tn(a1, e1).astype(BF16)
    g_qkv = jnp.stack([dot_tn(n1, d).astype(BF16) for d in (dq, dk, dv)])

    half_block = pl.BlockSpec((block, width), lambda i, *_: (i, 0))
    text_grad, sums0 = call(
        text_bwd_kernel, "text_bwd", (half,),
        [half_block, half_block, half_block, half_block, whole(gains.shape)],
        [(sd((own, width), F32), half_block), (sd((8, width), F32), whole((8, width)))],
        (text, dh1, part1_own, recv_dn1, gains))

    def all_reduce(value):
        rows_here = value.shape[0]
        mine = []
        for bit_a, bit_b in orders:
            perm = [(d * 2 + t, (d ^ (1 << (bit_a, bit_b)[t])) * 2 + t) for d in range(n_dp) for t in range(2)]
            bit = jnp.where(core == 0, dp >> bit_a, dp >> bit_b) & 1
            mine.append((perm, bit))
            rows_here //= 2
            send = lax.dynamic_slice_in_dim(value, (1 - bit) * rows_here, rows_here, axis=0)
            keep = lax.dynamic_slice_in_dim(value, bit * rows_here, rows_here, axis=0)
            got = lax.ppermute(send, ("dp", "tensor"), perm)
            value = (keep.astype(F32) + got.astype(F32)).astype(BF16)
        for perm, bit in reversed(mine):
            got = lax.ppermute(value, ("dp", "tensor"), perm)
            value = jnp.concatenate(
                [jnp.where(bit == 0, value, got), jnp.where(bit == 0, got, value)], axis=0)
        return value.astype(F32)

    def small_reduce(value, with_tensor):
        for bit, _ in orders:
            perm = [(d, d ^ (1 << bit)) for d in range(n_dp)]
            value = value + lax.ppermute(value, "dp", perm)
        return value + swap(value) if with_tensor else value

    ffn_out_grad = all_reduce(g_ffn_out)
    wide = hidden // 2
    r_in = all_reduce(jnp.concatenate([g_ffn_in[:, :wide], g_ffn_in[:, wide:]], axis=0))
    ffn_in_grad = jnp.concatenate([r_in[:width], r_in[width:]], axis=1)
    fold = lambda g: jnp.concatenate([g[: g.shape[0] // 2], g[g.shape[0] // 2 :]], axis=1)
    unfold = lambda g: jnp.concatenate([g[:, : g.shape[1] // 2], g[:, g.shape[1] // 2 :]], axis=0)
    r_cross = all_reduce(jnp.concatenate([g_cross_out, fold(g_cross_q), g_kv_own, g_kv_par], axis=0))
    cross_out_grad = r_cross[:local_width]
    cross_q_grad = unfold(r_cross[local_width : local_width + width // 2])
    base = local_width + width // 2
    kv_a, kv_b = r_cross[base : base + half_dv], r_cross[base + half_dv :]
    cross_kv_grad = jnp.concatenate(
        [jnp.where(core == 0, kv_a, kv_b), jnp.where(core == 0, kv_b, kv_a)], axis=0
    ).reshape(cross_kv.shape)
    r_self = all_reduce(jnp.concatenate([g_self_out, fold(g_qkv[0]), fold(g_qkv[1]), fold(g_qkv[2])], axis=0))
    self_out_grad = r_self[:local_width]
    hw = width // 2
    self_qkv_grad = jnp.stack(
        [unfold(r_self[local_width + j * hw : local_width + (j + 1) * hw]) for j in range(3)], axis=1)

    wide_sums = small_reduce(jnp.concatenate([sums0[0:2], sums1[0:3], sums2[0:4]], axis=0), True)
    gains_grad = jnp.stack([wide_sums[0], wide_sums[2], wide_sums[5]])
    shifts_grad = jnp.stack([wide_sums[1], wide_sums[3], wide_sums[6]])
    out_bias_grad = jnp.stack([wide_sums[4], wide_sums[7], wide_sums[8]])
    narrow = small_reduce(jnp.concatenate(
        [sums_in[0], sums_in[1], cross_q_bias, cross_v_bias, ffn_in_bias_grad[0]]), False)
    in_bias_grad = narrow[: 4 * local_width].reshape(4, local_width)
    ffn_in_bias_grad = narrow[4 * local_width :]

    return (layer_out, text_grad, patch_grad, gains_grad, shifts_grad, self_qkv_grad, in_bias_grad, self_out_grad,
            cross_q_grad, cross_kv_grad, cross_out_grad, ffn_in_grad, ffn_in_bias_grad, ffn_out_grad, out_bias_grad)


def bit_orders(mesh):
    n_dp = mesh.shape["dp"]
    bits = max(n_dp.bit_length() - 1, 0)
    third = (bits + 1) // 4 if bits else 0
    x_bits = list(range(0, third))
    y_bits = list(range(third, 2 * third))
    z_bits = list(range(2 * third, bits))
    return list(zip(x_bits + y_bits + z_bits, y_bits + x_bits + z_bits))


def solution(mesh):
    both = P(("dp", "tensor"), None)
    in_specs = (both, P("dp", None, "tensor"), P("dp", None), P("dp"), P(), P(), P(None, None, "tensor"),
                P(None, "tensor"), P("tensor", None), P(None, "tensor"), P(None, None, "tensor"), P("tensor", None),
                P(None, "tensor"), P("tensor"), P("tensor", None), P(), both)
    out_specs = (both, both, P("dp", None, "tensor"), P(), P(), P(None, None, "tensor"), P(None, "tensor"),
                 P("tensor", None), P(None, "tensor"), P(None, None, "tensor"), P("tensor", None), P(None, "tensor"),
                 P("tensor"), P("tensor", None), P())
    fn = functools.partial(local, mesh.shape["dp"], bit_orders(mesh))
    return jax.shard_map(fn, mesh=mesh, in_specs=in_specs, out_specs=out_specs, check_vma=False)
```

```python
import functools

import jax
import jax.numpy as jnp
from jax import lax
from jax.experimental import pallas as pl
from jax.experimental.pallas import tpu as pltpu
from jax.sharding import PartitionSpec as P

HEAD = 64
EPSILON = 1e-06
SCALE = 0.125
NEGATIVE = -1000000000.0
F32 = jnp.float32
BF16 = jnp.bfloat16
VMEM_BYTES = 60 * 1024 * 1024


def dot_nn(a, b):
    return lax.dot_general(a, b, (((1,), (0,)), ((), ())), preferred_element_type=F32)


def dot_nt(a, b):
    return lax.dot_general(a, b, (((1,), (1,)), ((), ())), preferred_element_type=F32)


def dot_tn(a, b):
    return lax.dot_general(a, b, (((0,), (0,)), ((), ())), preferred_element_type=F32)


def norm_parts(v):
    centre = v - jnp.mean(v, axis=-1, keepdims=True)
    spread = jnp.mean(centre * centre, axis=-1, keepdims=True)
    r = lax.rsqrt(spread + EPSILON)
    return centre * r, r


def norm_back(dn, y, r, gain):
    w = dn * gain
    return r * (w - jnp.mean(w, axis=-1, keepdims=True) - y * jnp.mean(w * y, axis=-1, keepdims=True))


def spread_heads(row, heads):
    column = lax.broadcasted_iota(jnp.int32, row.shape, 1) // HEAD
    return jnp.concatenate(
        [jnp.where(column == h, row, 0.0) for h in range(heads)], axis=0
    ).astype(BF16)


def join_heads(wide, length, heads):
    column = lax.broadcasted_iota(jnp.int32, (length, heads * HEAD), 1) // HEAD
    out = wide[0:length]
    for h in range(1, heads):
        out = jnp.where(column == h, wide[h * length : (h + 1) * length], out)
    return out


def softmax_columns(st):
    top = jnp.max(st, axis=0, keepdims=True)
    e = jnp.exp(st - top)
    return e / jnp.sum(e, axis=0, keepdims=True)


def self_fwd_kernel(rows, length, heads, half, xo, xp, gains, shifts, w, bias, wo, segk, segq,
                    n1, q, k, v, p, a, part):
    i = pl.program_id(0)
    x = jnp.where(i < half, xo[...].astype(F32), xp[...].astype(F32))
    y, _ = norm_parts(x)
    n = (y * gains[0:1, :].astype(F32) + shifts[0:1, :].astype(F32)).astype(BF16)
    n1[...] = n
    b = bias[...].astype(F32)
    qv = (dot_nn(n, w[0]) + b[0:1]).astype(BF16)
    kv = dot_nn(n, w[1]).astype(BF16)
    vv = (dot_nn(n, w[2]) + b[1:2]).astype(BF16)
    q[...] = qv
    k[...] = kv
    v[...] = vv
    qf, kf, vf = qv.astype(F32), kv.astype(F32), vv.astype(F32)
    outs = []
    for r in range(rows):
        at = slice(r * length, (r + 1) * length)
        kr = kf[at].astype(BF16)
        vr = vf[at].astype(BF16)
        st = dot_nt(kr, spread_heads(qf[at], heads)) * SCALE
        st = jnp.where(segk[r] == segq[r], st, NEGATIVE)
        pr = softmax_columns(st).astype(BF16)
        p[r] = pr
        outs.append(join_heads(dot_tn(pr, vr), length, heads))
    av = jnp.concatenate(outs, axis=0).astype(BF16)
    a[...] = av
    part[...] = dot_nn(av, wo[...]).astype(BF16)


def project_kernel(place, po, pp, w0, w1, bias, kv):
    for j in range(po.shape[0]):
        x = dot_nn(po[j], w0[...]) + dot_nn(pp[j], w1[...])
        kv[j] = (x + bias[...]).astype(BF16)


def cross_fwd_kernel(rows, length, heads, half, pick, xo, xp, part, recv, gains, shifts, bias, out_bias,
                     wq, kv, wo, h1, n2, c2, p, a, part2):
    i = pl.program_id(0)
    x = jnp.where(i < half, xo[...].astype(F32), xp[...].astype(F32))
    h = x + (part[...].astype(F32) + recv[...].astype(F32)) + out_bias[0:1, :].astype(F32)
    h1[...] = h
    y, _ = norm_parts(h)
    n = (y * gains[1:2, :].astype(F32) + shifts[1:2, :].astype(F32)).astype(BF16)
    n2[...] = n
    cv = (dot_nn(n, wq[...]) + bias[2:3, :].astype(F32)).astype(BF16)
    c2[...] = cv
    cf = cv.astype(F32)
    width = heads * HEAD
    outs = []
    for r in range(rows):
        at = slice(r * length, (r + 1) * length)
        im = pick[i * rows + r]
        kr = kv[im, :, 0:width]
        vr = kv[im, :, width : 2 * width]
        st = dot_nt(kr, spread_heads(cf[at], heads)) * SCALE
        pr = softmax_columns(st).astype(BF16)
        p[r] = pr
        outs.append(join_heads(dot_tn(pr, vr), length, heads))
    av = jnp.concatenate(outs, axis=0).astype(BF16)
    a[...] = av
    part2[...] = dot_nn(av, wo[...]).astype(BF16)


def ffn_send_kernel(half, bits, h1, part, recv, eo, ep, gains, shifts, out_bias, w_in, b_in, w_out,
                    h2, n3, e3, du, o_sum, g_sum, f_out, b_grad, acc):
    i = pl.program_id(0)
    h = h1[...] + (part[...].astype(F32) + recv[...].astype(F32)) + out_bias[1:2, :].astype(F32)
    h2[...] = h
    y, _ = norm_parts(h)
    n = (y * gains[2:3, :].astype(F32) + shifts[2:3, :].astype(F32)).astype(BF16)
    n3[...] = n
    e = jnp.where(i < half, eo[...].astype(F32), ep[...].astype(F32)).astype(BF16)
    e3[...] = e
    o, g = ffn_half(i, n, e, w_in, b_in, w_out, du, f_out, b_grad, acc)
    o_sum[...] = o.astype(BF16)
    g_sum[...] = g.astype(BF16)


def ffn_half(i, n, e, w_in, b_in, w_out, du, f_out, b_grad, acc):
    chunk = 384 if w_in.shape[1] % 384 == 0 else w_in.shape[1]
    last = i == pl.num_programs(0) - 1

    @pl.when(i == 0)
    def _():
        b_grad[...] = jnp.zeros_like(b_grad)
        acc[...] = jnp.zeros_like(acc)

    o_sum, g_sum = None, None
    for c in range(w_in.shape[1] // chunk):
        at = slice(c * chunk, (c + 1) * chunk)
        u = dot_nn(n, w_in[:, at]) + b_in[:, at].astype(F32)
        cdf = 0.5 * (1.0 + lax.erf(u * 0.7071067811865476))
        m = (u * cdf).astype(BF16)
        slope = cdf + u * (jnp.exp(-0.5 * u * u) * 0.3989422804014327)
        d = (dot_nt(e, w_out[at, :]) * slope).astype(BF16)
        du[:, at] = d
        b_grad[:, at] += jnp.sum(d.astype(F32), axis=0, keepdims=True)
        o = dot_nn(m, w_out[at, :])
        g = dot_nt(d, w_in[:, at])
        o_sum = o if o_sum is None else o_sum + o
        g_sum = g if g_sum is None else g_sum + g
        acc[at, :] += dot_tn(m, e)

    @pl.when(last)
    def _():
        f_out[...] = acc[...].astype(BF16)

    return o_sum, g_sum


def ffn_keep_kernel(half, bits, n3, e3, o_in, g_in, w_in, b_in, w_out,
                    du, part_own, part_par, pdn, f_out, b_grad, acc):
    i = pl.program_id(0)
    o, g = ffn_half(i, n3[...], e3[...], w_in, b_in, w_out, du, f_out, b_grad, acc)
    pdn[...] = (g + g_in[...].astype(F32)).astype(BF16)
    o = (o + o_in[...].astype(F32)).astype(BF16)

    @pl.when(i < half)
    def _():
        part_own[...] = o

    @pl.when(i >= half)
    def _():
        part_par[...] = o


def ffn_in_kernel(bits, n3, du_a, du_b, send, keep):
    n = n3[...]
    other = pl.program_id(1) != bits[0]

    @pl.when(pl.program_id(0) == 0)
    def _():
        @pl.when(other)
        def _():
            send[...] = dot_tn(n, du_a[...]).astype(BF16)

        @pl.when(jnp.logical_not(other))
        def _():
            send[...] = dot_tn(n, du_b[...]).astype(BF16)

    @pl.when(pl.program_id(0) == 1)
    def _():
        @pl.when(other)
        def _():
            keep[...] = dot_tn(n, du_a[...]).astype(BF16)

        @pl.when(jnp.logical_not(other))
        def _():
            keep[...] = dot_tn(n, du_b[...]).astype(BF16)


def cross_bwd_kernel(rows, length, heads, half, pick, h2, part, recv, eo, ep, gains, wo, c2, p, kv, wq, a2, n2,
                     dh2, dkv, pdn, sums, sums_in, g_out, g_q, dk_acc, dv_acc, dk_row, dv_row, dq_buf,
                     out_acc, q_acc):
    i = pl.program_id(0)
    width = heads * HEAD

    @pl.when(i == 0)
    def _():
        sums[...] = jnp.zeros_like(sums)
        sums_in[...] = jnp.zeros_like(sums_in)
        dk_acc[...] = jnp.zeros_like(dk_acc)
        dv_acc[...] = jnp.zeros_like(dv_acc)
        out_acc[...] = jnp.zeros_like(out_acc)
        q_acc[...] = jnp.zeros_like(q_acc)

    dn = part[...].astype(F32) + recv[...].astype(F32)
    y, rs = norm_parts(h2[...])
    g3 = jnp.where(i < half, eo[...].astype(F32), ep[...].astype(F32))
    d = g3 + norm_back(dn, y, rs, gains[2:3, :].astype(F32))
    dh2[...] = d
    e = d.astype(BF16)

    @pl.when(i < half)
    def _():
        sums[0:1, :] += jnp.sum(dn * y, axis=0, keepdims=True)
        sums[1:2, :] += jnp.sum(dn, axis=0, keepdims=True)
        sums[2:3, :] += jnp.sum(d, axis=0, keepdims=True)
        sums[3:4, :] += jnp.sum(g3, axis=0, keepdims=True)

    da = dot_nt(e, wo[...]).astype(BF16).astype(F32)
    cf = c2[...].astype(F32)
    for r in range(rows):
        at = slice(r * length, (r + 1) * length)
        im = pick[i * rows + r]
        kr = kv[im, :, 0:width]
        vr = kv[im, :, width : 2 * width]
        pr = p[r]
        wide_o = spread_heads(da[at], heads)
        dpt = dot_nt(vr, wide_o)
        dv_row[r] = dot_nn(pr, wide_o)
        pf = pr.astype(F32)
        ds = (pf * (dpt - jnp.sum(pf * dpt, axis=0, keepdims=True))).astype(BF16)
        dq_buf[at, :] = join_heads(dot_tn(ds, kr), length, heads)
        dk_row[r] = dot_nn(ds, spread_heads(cf[at], heads))
    dc = (dq_buf[...] * SCALE).astype(BF16)
    pdn[...] = dot_nt(dc, wq[...]).astype(BF16)
    sums_in[0:1, :] += jnp.sum(dc.astype(F32), axis=0, keepdims=True)
    out_acc[...] += dot_tn(a2[...], e)
    q_acc[...] += dot_tn(n2[...], dc)
    for r in range(rows):
        im = pick[i * rows + r]
        dk_acc[im] += dk_row[r]
        dv_acc[im] += dv_row[r]

    @pl.when(i == pl.num_programs(0) - 1)
    def _():
        total = None
        for j in range(dkv.shape[0]):
            dkv[j, :, 0:width] = (dk_acc[j] * SCALE).astype(BF16)
            low = dv_acc[j].astype(BF16)
            dkv[j, :, width : 2 * width] = low
            s = jnp.sum(low.astype(F32), axis=0, keepdims=True)
            total = s if total is None else total + s
        sums_in[1:2, :] = total
        g_out[...] = out_acc[...].astype(BF16)
        fold = q_acc.shape[0] // 2
        g_q[:, 0:width] = q_acc[0:fold, :].astype(BF16)
        g_q[:, width : 2 * width] = q_acc[fold : 2 * fold, :].astype(BF16)


def kv_grad_kernel(bits, po, pp, dkv, w_own, w_par, g_out, g_q, send, keep, terms_own, terms_par, own_acc, par_acc):
    i = pl.program_id(0)

    @pl.when(i == 0)
    def _():
        own_acc[...] = jnp.zeros_like(own_acc)
        par_acc[...] = jnp.zeros_like(par_acc)

    for j in range(po.shape[0]):
        d = dkv[j]
        own_acc[...] += dot_tn(po[j], d)
        par_acc[...] += dot_tn(pp[j], d)
        terms_own[j] = dot_nt(d, w_own[...]).astype(BF16)
        terms_par[j] = dot_nt(d, w_par[...]).astype(BF16)

    @pl.when(i == pl.num_programs(0) - 1)
    def _():
        cut = g_out.shape[0]

        @pl.when(bits[0] == 0)
        def _():
            keep[0:cut, :] = g_out[...]
            keep[cut:, :] = own_acc[...].astype(BF16)
            send[0:cut, :] = g_q[...]
            send[cut:, :] = par_acc[...].astype(BF16)

        @pl.when(bits[0] != 0)
        def _():
            send[0:cut, :] = g_out[...]
            send[cut:, :] = own_acc[...].astype(BF16)
            keep[0:cut, :] = g_q[...]
            keep[cut:, :] = par_acc[...].astype(BF16)


def self_bwd_kernel(rows, length, heads, half, bits, h1, dh2, part, recv, xo, xp, gains, wo, q, k, v, p, w, a1, n1,
                    sums2, sums_in2, b_grad_a, b_grad_b,
                    dh1, part_own, part_par, send, keep, q_buf, k_buf, v_buf, out_acc, w_acc, sums, sums_in):
    i = pl.program_id(0)
    width = heads * HEAD

    @pl.when(i == 0)
    def _():
        sums[...] = jnp.zeros_like(sums)
        sums_in[...] = jnp.zeros_like(sums_in)
        out_acc[...] = jnp.zeros_like(out_acc)
        w_acc[...] = jnp.zeros_like(w_acc)

    dn = part[...].astype(F32) + recv[...].astype(F32)
    y, rs = norm_parts(h1[...])
    d = dh2[...] + norm_back(dn, y, rs, gains[1:2, :].astype(F32))
    e = d.astype(BF16)

    @pl.when(i < half)
    def _():
        dh1[...] = d
        sums[2:3, :] += jnp.sum(dn * y, axis=0, keepdims=True)
        sums[3:4, :] += jnp.sum(dn, axis=0, keepdims=True)
        sums[4:5, :] += jnp.sum(d, axis=0, keepdims=True)

    da = dot_nt(e, wo[...]).astype(BF16).astype(F32)
    qf, kf, vf = q[...].astype(F32), k[...].astype(F32), v[...].astype(F32)
    for r in range(rows):
        at = slice(r * length, (r + 1) * length)
        kr = kf[at].astype(BF16)
        vr = vf[at].astype(BF16)
        pr = p[r]
        wide_o = spread_heads(da[at], heads)
        dpt = dot_nt(vr, wide_o)
        v_buf[at, :] = dot_nn(pr, wide_o)
        pf = pr.astype(F32)
        ds = (pf * (dpt - jnp.sum(pf * dpt, axis=0, keepdims=True))).astype(BF16)
        q_buf[at, :] = join_heads(dot_tn(ds, kr), length, heads)
        k_buf[at, :] = dot_nn(ds, spread_heads(qf[at], heads))
    dqv = (q_buf[...] * SCALE).astype(BF16)
    dkv = (k_buf[...] * SCALE).astype(BF16)
    dvv = v_buf[...].astype(BF16)
    sums_in[0:1, :] += jnp.sum(dqv.astype(F32), axis=0, keepdims=True)
    sums_in[1:2, :] += jnp.sum(dvv.astype(F32), axis=0, keepdims=True)
    back = dot_nt(dqv, w[0]) + dot_nt(dkv, w[1]) + dot_nt(dvv, w[2])
    low = back.astype(BF16)

    @pl.when(i < half)
    def _():
        part_own[...] = low

    @pl.when(i >= half)
    def _():
        part_par[...] = low

    x = jnp.where(i < half, xo[...].astype(F32), xp[...].astype(F32))
    y0, _ = norm_parts(x)
    sums[0:1, :] += jnp.sum(back * y0, axis=0, keepdims=True)
    sums[1:2, :] += jnp.sum(back, axis=0, keepdims=True)
    out_acc[...] += dot_tn(a1[...], e)
    n = n1[...]
    w_acc[0] += dot_tn(n, dqv)
    w_acc[1] += dot_tn(n, dkv)
    w_acc[2] += dot_tn(n, dvv)

    @pl.when(i == pl.num_programs(0) - 1)
    def _():
        cut = out_acc.shape[0]
        fold = w_acc.shape[1] // 2
        extra = (send.shape[0] - 2 * cut)

        def folded(ref, base, j):
            ref[base : base + fold, 0:width] = w_acc[j, 0:fold, :].astype(BF16)
            ref[base : base + fold, width : 2 * width] = w_acc[j, fold : 2 * fold, :].astype(BF16)

        def first(ref):
            ref[0:cut, :] = out_acc[...].astype(BF16)
            folded(ref, cut, 0)
            pad = jnp.zeros((extra - 16, 2 * width), F32)
            ref[2 * cut :, :] = jnp.concatenate([sums[0:8, :], sums2[0:8, :], pad], axis=0).astype(BF16)

        def second(ref):
            folded(ref, 0, 1)
            folded(ref, fold, 2)
            rows_in = jnp.concatenate([sums_in[0:8, :], sums_in2[0:8, :]], axis=0)
            left = jnp.concatenate([rows_in, jnp.zeros_like(rows_in)], axis=1)
            low, high = jnp.where(bits[2] == 0, b_grad_b[...], b_grad_a[...]), jnp.where(
                bits[2] == 0, b_grad_a[...], b_grad_b[...])
            bias_rows = jnp.concatenate(
                [low, high, jnp.zeros((extra - 18, 2 * width), F32)], axis=0)
            ref[2 * fold :, :] = jnp.concatenate([left, bias_rows], axis=0).astype(BF16)

        @pl.when(bits[0] == 0)
        def _():
            first(keep)
            second(send)

        @pl.when(bits[0] != 0)
        def _():
            first(send)
            second(keep)


def text_bwd_kernel(x, dh1, part, recv, gains, out):
    dn = part[...].astype(F32) + recv[...].astype(F32)
    y, rs = norm_parts(x[...].astype(F32))
    out[...] = dh1[...] + norm_back(dn, y, rs, gains[0:1, :].astype(F32))


def widen_kernel(bits, mine, got, out):
    out[...] = jnp.where(pl.program_id(0) == bits[0], mine[...].astype(F32), got[...].astype(F32))


def open_cross_kernel(cut, bits, mine, got, g_out, g_q, g_kv):
    width = g_q.shape[1]
    zero = bits[0] == 0
    core = bits[1]
    deep = mine.shape[0] - cut
    g_out[...] = jnp.where(zero, mine[0:cut, :].astype(F32), got[0:cut, :].astype(F32))
    q = jnp.where(zero, got[0:cut, :].astype(F32), mine[0:cut, :].astype(F32))
    fold = q.shape[0]
    g_q[0:fold, :] = q[:, 0:width]
    g_q[fold : 2 * fold, :] = q[:, width : 2 * width]
    swapped = jnp.logical_xor(zero, core == 0)
    g_kv[0:deep, :] = jnp.where(swapped, got[cut:, :].astype(F32), mine[cut:, :].astype(F32))
    g_kv[deep : 2 * deep, :] = jnp.where(swapped, mine[cut:, :].astype(F32), got[cut:, :].astype(F32))


def open_self_kernel(cut, fold, bits, mine, got, g_out, g_w, rows_a, rows_b):
    zero = bits[0] == 0
    width = g_w.shape[2]

    def first(at):
        return jnp.where(zero, mine[at, :].astype(F32), got[at, :].astype(F32))

    def second(at):
        return jnp.where(zero, got[at, :].astype(F32), mine[at, :].astype(F32))

    def unfold(j, v):
        g_w[j, 0:fold, :] = v[:, 0:width]
        g_w[j, fold : 2 * fold, :] = v[:, width : 2 * width]

    g_out[...] = first(slice(0, cut))
    unfold(0, first(slice(cut, cut + fold)))
    unfold(1, second(slice(0, fold)))
    unfold(2, second(slice(fold, 2 * fold)))
    rows_a[...] = first(slice(2 * cut, mine.shape[0]))
    rows_b[...] = second(slice(2 * fold, mine.shape[0]))


def whole(shape):
    zeros = (0,) * len(shape)
    return pl.BlockSpec(shape, lambda *_: zeros)


def call(kernel, name, grid, ins, outs, args, scratch=(), prefetch=0, flops=0, exps=0):
    moved = sum(a.size * a.dtype.itemsize for a in args) + sum(
        functools.reduce(lambda u, v: u * v, s.shape, 1) * s.dtype.itemsize for s, _ in outs
    )
    return pl.pallas_call(
        kernel,
        out_shape=[s for s, _ in outs],
        grid_spec=pltpu.PrefetchScalarGridSpec(
            num_scalar_prefetch=prefetch,
            grid=grid,
            in_specs=list(ins),
            out_specs=[b for _, b in outs],
            scratch_shapes=list(scratch),
        ),
        compiler_params=pltpu.CompilerParams(vmem_limit_bytes=VMEM_BYTES),
        cost_estimate=pl.CostEstimate(flops=flops, transcendentals=exps, bytes_accessed=moved),
        name=name,
    )(*args)


def local(n_dp, plans, text, patches, segment_ids, image_of_row, gains, shifts, self_qkv, in_bias, self_out,
          cross_q, cross_kv, cross_out, ffn_in, ffn_in_bias, ffn_out, out_bias, cotangent):
    core = lax.axis_index("tensor")
    dp = lax.axis_index("dp")
    own, width = text.shape
    tokens = 2 * own
    rows, length = segment_ids.shape
    local_width = self_out.shape[0]
    heads = local_width // HEAD
    images, spots, half_dv = patches.shape
    hidden = ffn_in.shape[1]
    wide = hidden // 2
    block_rows = rows // 2
    block = block_rows * length
    steps = tokens // block
    half = steps // 2
    sd = jax.ShapeDtypeStruct

    swap = lambda v: lax.ppermute(v, "tensor", [(0, 1), (1, 0)])
    text_par = swap(text)
    cot_par = swap(cotangent)
    patches_par = swap(patches)

    def bit_of(level):
        return jnp.where(core == 0, dp >> level[0], dp >> level[1]) & 1

    def send_along(value, level):
        perm = [(d * 2 + t, (d ^ (1 << level[t])) * 2 + t) for d in range(n_dp) for t in range(2)]
        return lax.ppermute(value, ("dp", "tensor"), perm)

    def add(a, b):
        return (a.astype(F32) + b.astype(F32)).astype(BF16)

    def after(value, *others):
        return lax.optimization_barrier((value,) + others)[0]

    def reduce_chain(send, keep, plan):
        halving, doubling = plan
        got = yield send, halving[0]
        keep = keep()
        for level in halving[1:]:
            n = keep.shape[0] // 2
            bit = bit_of(level)
            cut = lambda v, b: lax.dynamic_slice_in_dim(v, b * n, n, axis=0)
            send = add(cut(keep, 1 - bit), cut(got, 1 - bit))
            keep = add(cut(keep, bit), cut(got, bit))
            got = yield send, level
        value = add(keep, got)
        for level in doubling:
            got = yield value, level
            value = add(value, got)
        for level in reversed(halving[1:]):
            got = yield value, level
            place = lax.broadcasted_iota(jnp.int32, (2,) + value.shape, 0)
            value = jnp.where(place == bit_of(level), value[None], got[None]).reshape(-1, value.shape[1])
        got = yield value, halving[0]
        return value, got

    class Chain:
        def __init__(self, send, keep, plan):
            self.steps = reduce_chain(send, keep, plan)
            self.result = None
            self.sent, level = next(self.steps)
            self.got = send_along(self.sent, level)

        def advance(self, *hold):
            if self.result is not None:
                return
            got = after(self.got, *hold) if hold else self.got
            try:
                self.sent, level = self.steps.send(got)
                self.got = send_along(self.sent, level)
            except StopIteration as stop:
                self.result = stop.value

        def finish(self):
            while self.result is None:
                self.advance()
            return self.result

    first_bits = [
        jnp.stack([bit_of(plan[0][0]), core, bit_of(plans[0][0][0])]).astype(jnp.int32) for plan in plans]
    bits_out, bits_in, bits_cross, bits_self = first_bits

    w3 = jnp.transpose(self_qkv, (1, 0, 2))
    wkv = cross_kv.reshape(cross_kv.shape[0], 2 * local_width)
    flip = lambda v: jnp.where(core == 0, v, jnp.roll(v, rows // 2, axis=0))
    seg = flip(segment_ids)
    pick = flip(image_of_row)
    segk = seg[:, :, None]
    segq = jnp.tile(seg, (1, heads))[:, None, :]

    tok = lambda n: pl.BlockSpec((block, n), lambda i, *_: (i, 0))
    tok_other = lambda n: pl.BlockSpec((block, n), lambda i, *_: ((i + half) % steps, 0))
    tok_own = lambda n: pl.BlockSpec((block, n), lambda i, *_: (jnp.minimum(i, half - 1), 0))
    tok_par = lambda n: pl.BlockSpec((block, n), lambda i, *_: (jnp.maximum(i - half, 0), 0))
    row3 = lambda a, b: pl.BlockSpec((block_rows, a, b), lambda i, *_: (i, 0, 0))
    act = lambda n, dt=BF16: (sd((tokens, n), dt), tok(n))
    full = lambda shape, dt=BF16: (sd(shape, dt), whole(shape))
    ql = heads * length
    sizes = (block_rows, length, heads, half)

    n1, q, k, v, p1, a1, part1 = call(
        functools.partial(self_fwd_kernel, *sizes), "self_fwd", (steps,),
        [tok_own(width), tok_par(width), whole(gains.shape), whole(shifts.shape), whole(w3.shape),
         whole(in_bias.shape), whole(self_out.shape), row3(length, 1), row3(1, ql)],
        [act(width), act(local_width), act(local_width), act(local_width),
         (sd((rows, length, ql), BF16), row3(length, ql)), act(local_width), act(width)],
        (text, text_par, gains, shifts, w3, in_bias, self_out, segk, segq),
        flops=2 * tokens * width * 4 * local_width, exps=rows * length * ql)
    recv1 = swap(part1)

    kv_bias = jnp.concatenate([jnp.zeros((local_width,), F32), in_bias[3].astype(F32)])[None, :]
    place = jnp.full((1,), core, jnp.int32)
    group = 3 if images % 3 == 0 else 1
    image_block = lambda n: pl.BlockSpec((group, spots, n), lambda i, *_: (i, 0, 0))
    (kv,) = call(
        project_kernel, "project", (images // group,),
        [image_block(half_dv), image_block(half_dv),
         pl.BlockSpec((half_dv, 2 * local_width), lambda i, c: (c[0], 0)),
         pl.BlockSpec((half_dv, 2 * local_width), lambda i, c: (1 - c[0], 0)),
         whole(kv_bias.shape)],
        [(sd((images, spots, 2 * local_width), BF16), image_block(2 * local_width))],
        (place, patches, patches_par, wkv, wkv, kv_bias), prefetch=1,
        flops=4 * images * spots * 2 * half_dv * local_width)

    h1, n2, c2, p2, a2, part2 = call(
        functools.partial(cross_fwd_kernel, *sizes), "cross_fwd", (steps,),
        [tok_own(width), tok_par(width), tok(width), tok_other(width), whole(gains.shape), whole(shifts.shape),
         whole(in_bias.shape), whole(out_bias.shape), whole(cross_q.shape), whole(kv.shape), whole(cross_out.shape)],
        [act(width, F32), act(width), act(local_width), (sd((rows, spots, ql), BF16), row3(spots, ql)),
         act(local_width), act(width)],
        (pick, text, text_par, part1, recv1, gains, shifts, in_bias, out_bias, cross_q, kv, cross_out), prefetch=1,
        flops=2 * tokens * width * 2 * local_width + 4 * rows * ql * spots * local_width, exps=rows * ql * spots)
    recv2 = swap(part2)

    own_spec = lambda n: (sd((own, n), BF16), tok_own(n))
    par_spec = lambda n: (sd((own, n), BF16), tok_par(n))
    b_in = ffn_in_bias[None, :]
    half_specs = lambda at: [
        pl.BlockSpec((width, wide), lambda i, b: (0, at(b[0]))),
        pl.BlockSpec((1, wide), lambda i, b: (0, at(b[0]))),
        pl.BlockSpec((wide, width), lambda i, b: (at(b[0]), 0))]
    ffn_acc = [pltpu.VMEM((wide, width), F32)]
    ffn_cost = dict(flops=5 * tokens * width * hidden, exps=tokens * hidden)
    h2, n3, e3, du_a, o_sum, g_sum, out_send, b_grad_a = call(
        functools.partial(ffn_send_kernel, half), "ffn_send", (steps,),
        [tok(width), tok(width), tok_other(width), tok_own(width), tok_par(width), whole(gains.shape),
         whole(shifts.shape), whole(out_bias.shape)] + half_specs(lambda b: 1 - b),
        [act(width, F32), act(width), act(width), act(wide), act(width), act(width), full((wide, width)),
         full((1, wide), F32)],
        (bits_out, h1, part2, recv2, cotangent, cot_par, gains, shifts, out_bias, ffn_in, b_in, ffn_out),
        scratch=ffn_acc, prefetch=1, **ffn_cost)
    chain_out = Chain(out_send, lambda: out_keep, plans[0])
    du_b, part3_own, part3_par, pdn3, out_keep, b_grad_b = call(
        functools.partial(ffn_keep_kernel, half), "ffn_keep", (steps,),
        [tok(width), tok(width), tok(width), tok(width)] + half_specs(lambda b: b),
        [act(wide), own_spec(width), par_spec(width), act(width), full((wide, width)), full((1, wide), F32)],
        (after(bits_out, out_send), n3, e3, o_sum, g_sum, ffn_in, b_in, ffn_out),
        scratch=ffn_acc, prefetch=1, **ffn_cost)
    recv3 = swap(pdn3)
    chain_out.advance(pdn3)
    recv_out = swap(part3_par)
    layer_out = h2[:own] + (part3_own.astype(F32) + recv_out.astype(F32)) + out_bias[2].astype(F32)

    hw = width // 2
    bits_dw = jnp.stack([bits_out[0], bits_in[0]])
    in_send, in_keep = call(
        ffn_in_kernel, "ffn_in_grad", (2, 2),
        [pl.BlockSpec((tokens, hw), lambda j, c, b: (0, jnp.where(j == 0, 1 - b[1], b[1]))),
         whole((tokens, wide)), whole((tokens, wide))],
        [(sd((width, wide), BF16), pl.BlockSpec((hw, wide), lambda j, c, b: (jnp.where(j == 0, c, 1), 0))),
         (sd((width, wide), BF16), pl.BlockSpec((hw, wide), lambda j, c, b: (jnp.where(j == 0, 0, c), 0)))],
        (after(bits_dw, chain_out.sent, pdn3), n3, du_a, du_b), prefetch=1, flops=2 * tokens * width * hidden)

    chain_in = Chain(in_send, lambda: in_keep, plans[1])
    chain_out.advance(in_send)
    dh2, dkv, pdn2, sums2, sums_in2, g_cross_out, g_cross_q = call(
        functools.partial(cross_bwd_kernel, *sizes), "cross_bwd", (steps,),
        [tok(width), tok(width), tok_other(width), tok_own(width), tok_par(width), whole(gains.shape),
         whole(cross_out.shape), tok(local_width), row3(spots, ql), whole(kv.shape), whole(cross_q.shape),
         tok(local_width), tok(width)],
        [act(width, F32), full(kv.shape), act(width), full((8, width), F32), full((8, local_width), F32),
         full((local_width, width)), full((hw, width))],
        (after(pick, chain_in.sent, chain_out.sent), h2, pdn3, recv3, cotangent, cot_par, gains, cross_out, c2, p2, kv, cross_q, a2, n2), prefetch=1,
        scratch=[pltpu.VMEM((images, spots, local_width), F32)] * 2
        + [pltpu.VMEM((block_rows, spots, local_width), F32)] * 2
        + [pltpu.VMEM((block, local_width), F32), pltpu.VMEM((local_width, width), F32),
           pltpu.VMEM((width, local_width), F32)],
        flops=2 * tokens * width * 4 * local_width + 8 * rows * ql * spots * local_width)
    recv_dn2 = swap(pdn2)
    chain_out.advance(pdn2)
    chain_in.advance(pdn2)

    deep = local_width + half_dv
    cross_send, cross_keep, terms_own, terms_par = call(
        kv_grad_kernel, "kv_grad", (images // group,),
        [image_block(half_dv), image_block(half_dv), image_block(2 * local_width),
         pl.BlockSpec((half_dv, 2 * local_width), lambda i, c: (c[1], 0)),
         pl.BlockSpec((half_dv, 2 * local_width), lambda i, c: (1 - c[1], 0)),
         whole(g_cross_out.shape), whole(g_cross_q.shape)],
        [full((deep, width)), full((deep, width)),
         (sd(patches.shape, BF16), image_block(half_dv)), (sd(patches.shape, BF16), image_block(half_dv))],
        (after(bits_cross, chain_in.sent, chain_out.sent), patches, patches_par, dkv, wkv, wkv, g_cross_out, g_cross_q), prefetch=1,
        scratch=[pltpu.VMEM((half_dv, width), F32)] * 2,
        flops=8 * images * spots * 2 * half_dv * local_width)
    chain_cross = Chain(cross_send, lambda: cross_keep, plans[2])
    chain_out.advance(cross_send)
    chain_in.advance(cross_send)
    patch_grad = terms_own.astype(F32) + swap(terms_par).astype(F32)

    extra = 32
    tall = 2 * local_width + extra
    dh1, part1_own, part1_par, self_send, self_keep = call(
        functools.partial(self_bwd_kernel, *sizes), "self_bwd", (steps,),
        [tok(width), tok(width), tok(width), tok_other(width), tok_own(width), tok_par(width), whole(gains.shape),
         whole(self_out.shape), tok(local_width), tok(local_width), tok(local_width), row3(length, ql),
         whole(w3.shape), tok(local_width), tok(width), whole((8, width)), whole((8, local_width)),
         whole((1, wide)), whole((1, wide))],
        [(sd((own, width), F32), tok_own(width)), own_spec(width), par_spec(width), full((tall, width)),
         full((tall, width))],
        (after(bits_self, chain_in.sent, chain_out.sent, chain_cross.sent), h1, dh2, pdn2, recv_dn2, text, text_par, gains, self_out, q, k, v, p1, w3, a1, n1, sums2,
         sums_in2, b_grad_a, b_grad_b), prefetch=1,
        scratch=[pltpu.VMEM((block, local_width), F32)] * 3
        + [pltpu.VMEM((local_width, width), F32), pltpu.VMEM((3, width, local_width), F32),
           pltpu.VMEM((8, width), F32), pltpu.VMEM((8, local_width), F32)],
        flops=2 * tokens * width * 8 * local_width)
    recv_dn1 = swap(part1_par)
    chain_self = Chain(self_send, lambda: self_keep, plans[3])
    chains = [chain_cross, chain_in, chain_out, chain_self]
    for chain in chains[:3]:
        chain.advance(self_send)

    text_block = own // 2
    half_block = pl.BlockSpec((text_block, width), lambda i, *_: (i, 0))
    (text_grad,) = call(
        text_bwd_kernel, "text_bwd", (2,),
        [half_block, half_block, half_block, half_block, whole(gains.shape)],
        [(sd((own, width), F32), half_block)],
        (text, dh1, part1_own, recv_dn1, gains))

    out_mine, out_got = chain_out.finish()
    in_mine, in_got = chain_in.finish()
    cross_mine, cross_got = chain_cross.finish()
    self_mine, self_got = chain_self.finish()

    piece = pl.BlockSpec((hw, width), lambda j, c, b: (c, 0))
    (ffn_out_grad,) = call(
        widen_kernel, "open_ffn_out", (2, wide // hw), [piece, piece],
        [(sd((hidden, width), F32), pl.BlockSpec((hw, width), lambda j, c, b: (j * (wide // hw) + c, 0)))],
        (bits_out, out_mine, out_got), prefetch=1)
    (ffn_in_grad,) = call(
        widen_kernel, "open_ffn_in", (2, 2), [piece, piece],
        [(sd((width, hidden), F32), pl.BlockSpec((hw, wide), lambda j, c, b: (j, c)))],
        (bits_in, in_mine, in_got), prefetch=1)
    cross_out_grad, cross_q_grad, kv_grad = call(
        functools.partial(open_cross_kernel, local_width), "open_cross", (1,),
        [whole((deep, width)), whole((deep, width))],
        [full((local_width, width), F32), full((width, local_width), F32), full((2 * half_dv, width), F32)],
        (bits_cross, cross_mine, cross_got), prefetch=1)
    cross_kv_grad = kv_grad.reshape(cross_kv.shape)
    self_out_grad, qkv_grad, rows_a, rows_b = call(
        functools.partial(open_self_kernel, local_width, hw), "open_self", (1,),
        [whole((tall, width)), whole((tall, width))],
        [full((local_width, width), F32), full((3, width, local_width), F32), full((extra, width), F32),
         full((extra, width), F32)],
        (bits_self, self_mine, self_got), prefetch=1)
    self_qkv_grad = jnp.transpose(qkv_grad, (1, 0, 2))

    rows_a = rows_a[0:12] + swap(rows_a[0:12])
    gains_grad = jnp.stack([rows_a[0], rows_a[2], rows_a[8]])
    shifts_grad = jnp.stack([rows_a[1], rows_a[3], rows_a[9]])
    out_bias_grad = jnp.stack([rows_a[4], rows_a[10], rows_a[11]])
    in_bias_grad = jnp.concatenate([rows_b[0:2, :local_width], rows_b[8:10, :local_width]], axis=0)
    ffn_in_bias_grad = jnp.concatenate([rows_b[16], rows_b[17]])

    return (layer_out, text_grad, patch_grad, gains_grad, shifts_grad, self_qkv_grad, in_bias_grad, self_out_grad,
            cross_q_grad, cross_kv_grad, cross_out_grad, ffn_in_grad, ffn_in_bias_grad, ffn_out_grad, out_bias_grad)


def make_plans(mesh):
    bits = mesh.shape["dp"].bit_length() - 1
    third = (bits + 1) // 4
    x, y, z = list(range(third)), list(range(third, 2 * third)), list(range(2 * third, bits))
    flat = list(zip(x + y, y + x))
    up = list(zip(z, z))
    return [(flat + up[:1], up[1:])] * 4


def solution(mesh):
    both = P(("dp", "tensor"), None)
    in_specs = (both, P("dp", None, "tensor"), P("dp", None), P("dp"), P(), P(), P(None, None, "tensor"),
                P(None, "tensor"), P("tensor", None), P(None, "tensor"), P(None, None, "tensor"), P("tensor", None),
                P(None, "tensor"), P("tensor"), P("tensor", None), P(), both)
    out_specs = (both, both, P("dp", None, "tensor"), P(), P(), P(None, None, "tensor"), P(None, "tensor"),
                 P("tensor", None), P(None, "tensor"), P(None, None, "tensor"), P("tensor", None), P(None, "tensor"),
                 P("tensor"), P("tensor", None), P())
    fn = functools.partial(local, mesh.shape["dp"], make_plans(mesh))
    return jax.shard_map(fn, mesh=mesh, in_specs=in_specs, out_specs=out_specs, check_vma=False)
```

```python
import functools

import jax
import jax.numpy as jnp
from jax import lax
from jax.experimental import pallas as pl
from jax.experimental.pallas import tpu as pltpu
from jax.sharding import PartitionSpec as P

HEAD = 64
EPSILON = 1e-06
SCALE = 0.125
NEGATIVE = -1000000000.0
F32 = jnp.float32
BF16 = jnp.bfloat16
VMEM_BYTES = 60 * 1024 * 1024


def dot_nn(a, b):
    return lax.dot_general(a, b, (((1,), (0,)), ((), ())), preferred_element_type=F32)


def dot_nt(a, b):
    return lax.dot_general(a, b, (((1,), (1,)), ((), ())), preferred_element_type=F32)


def dot_tn(a, b):
    return lax.dot_general(a, b, (((0,), (0,)), ((), ())), preferred_element_type=F32)


def norm_parts(v):
    centre = v - jnp.mean(v, axis=-1, keepdims=True)
    spread = jnp.mean(centre * centre, axis=-1, keepdims=True)
    r = lax.rsqrt(spread + EPSILON)
    return centre * r, r


def norm_back(dn, y, r, gain):
    w = dn * gain
    return r * (w - jnp.mean(w, axis=-1, keepdims=True) - y * jnp.mean(w * y, axis=-1, keepdims=True))


def spread_heads(row, heads):
    column = lax.broadcasted_iota(jnp.int32, row.shape, 1) // HEAD
    return jnp.concatenate(
        [jnp.where(column == h, row, 0.0) for h in range(heads)], axis=0
    ).astype(BF16)


def join_heads(wide, length, heads):
    column = lax.broadcasted_iota(jnp.int32, (length, heads * HEAD), 1) // HEAD
    out = wide[0:length]
    for h in range(1, heads):
        out = jnp.where(column == h, wide[h * length : (h + 1) * length], out)
    return out


def softmax_columns(st):
    top = jnp.max(st, axis=0, keepdims=True)
    e = jnp.exp(st - top)
    return e / jnp.sum(e, axis=0, keepdims=True)


def self_fwd_kernel(rows, length, heads, half, xo, xp, gains, shifts, w, bias, wo, segk, segq,
                    n1, q, k, v, p, a, part):
    i = pl.program_id(0)
    x = jnp.where(i < half, xo[...].astype(F32), xp[...].astype(F32))
    y, _ = norm_parts(x)
    n = (y * gains[0:1, :].astype(F32) + shifts[0:1, :].astype(F32)).astype(BF16)
    n1[...] = n
    b = bias[...].astype(F32)
    qv = (dot_nn(n, w[0]) + b[0:1]).astype(BF16)
    kv = dot_nn(n, w[1]).astype(BF16)
    vv = (dot_nn(n, w[2]) + b[1:2]).astype(BF16)
    q[...] = qv
    k[...] = kv
    v[...] = vv
    qf, kf, vf = qv.astype(F32), kv.astype(F32), vv.astype(F32)
    outs = []
    for r in range(rows):
        at = slice(r * length, (r + 1) * length)
        kr = kf[at].astype(BF16)
        vr = vf[at].astype(BF16)
        st = dot_nt(kr, spread_heads(qf[at], heads)) * SCALE
        st = jnp.where(segk[r] == segq[r], st, NEGATIVE)
        pr = softmax_columns(st).astype(BF16)
        p[r] = pr
        outs.append(join_heads(dot_tn(pr, vr), length, heads))
    av = jnp.concatenate(outs, axis=0).astype(BF16)
    a[...] = av
    part[...] = dot_nn(av, wo[...]).astype(BF16)


def project_kernel(place, po, pp, w0, w1, bias, kv):
    for j in range(po.shape[0]):
        x = dot_nn(po[j], w0[...]) + dot_nn(pp[j], w1[...])
        kv[j] = (x + bias[...]).astype(BF16)


def cross_fwd_kernel(rows, length, heads, half, pick, xo, xp, part, recv, gains, shifts, bias, out_bias,
                     wq, kv, wo, h1, n2, c2, p, a, part2):
    i = pl.program_id(0)
    x = jnp.where(i < half, xo[...].astype(F32), xp[...].astype(F32))
    h = x + (part[...].astype(F32) + recv[...].astype(F32)) + out_bias[0:1, :].astype(F32)
    h1[...] = h
    y, _ = norm_parts(h)
    n = (y * gains[1:2, :].astype(F32) + shifts[1:2, :].astype(F32)).astype(BF16)
    n2[...] = n
    cv = (dot_nn(n, wq[...]) + bias[2:3, :].astype(F32)).astype(BF16)
    c2[...] = cv
    cf = cv.astype(F32)
    width = heads * HEAD
    outs = []
    for r in range(rows):
        at = slice(r * length, (r + 1) * length)
        im = pick[i * rows + r]
        kr = kv[im, :, 0:width]
        vr = kv[im, :, width : 2 * width]
        st = dot_nt(kr, spread_heads(cf[at], heads)) * SCALE
        pr = softmax_columns(st).astype(BF16)
        p[r] = pr
        outs.append(join_heads(dot_tn(pr, vr), length, heads))
    av = jnp.concatenate(outs, axis=0).astype(BF16)
    a[...] = av
    part2[...] = dot_nn(av, wo[...]).astype(BF16)


def ffn_send_kernel(half, bits, h1, part, recv, eo, ep, gains, shifts, out_bias, w_in, b_in, w_out,
                    h2, n3, e3, du, o_sum, g_sum, f_out, b_grad, acc):
    i = pl.program_id(0)
    h = h1[...] + (part[...].astype(F32) + recv[...].astype(F32)) + out_bias[1:2, :].astype(F32)
    h2[...] = h
    y, _ = norm_parts(h)
    n = (y * gains[2:3, :].astype(F32) + shifts[2:3, :].astype(F32)).astype(BF16)
    n3[...] = n
    e = jnp.where(i < half, eo[...].astype(F32), ep[...].astype(F32)).astype(BF16)
    e3[...] = e
    o, g = ffn_half(i, n, e, w_in, b_in, w_out, du, f_out, b_grad, acc)
    o_sum[...] = o.astype(BF16)
    g_sum[...] = g.astype(BF16)


def ffn_half(i, n, e, w_in, b_in, w_out, du, f_out, b_grad, acc):
    chunk = 384 if w_in.shape[1] % 384 == 0 else w_in.shape[1]
    last = i == pl.num_programs(0) - 1

    @pl.when(i == 0)
    def _():
        b_grad[...] = jnp.zeros_like(b_grad)
        acc[...] = jnp.zeros_like(acc)

    o_sum, g_sum = None, None
    for c in range(w_in.shape[1] // chunk):
        at = slice(c * chunk, (c + 1) * chunk)
        u = dot_nn(n, w_in[:, at]) + b_in[:, at].astype(F32)
        cdf = 0.5 * (1.0 + lax.erf(u * 0.7071067811865476))
        m = (u * cdf).astype(BF16)
        slope = cdf + u * (jnp.exp(-0.5 * u * u) * 0.3989422804014327)
        d = (dot_nt(e, w_out[at, :]) * slope).astype(BF16)
        du[:, at] = d
        b_grad[:, at] += jnp.sum(d.astype(F32), axis=0, keepdims=True)
        o = dot_nn(m, w_out[at, :])
        g = dot_nt(d, w_in[:, at])
        o_sum = o if o_sum is None else o_sum + o
        g_sum = g if g_sum is None else g_sum + g
        acc[at, :] += dot_tn(m, e)

    @pl.when(last)
    def _():
        f_out[...] = acc[...].astype(BF16)

    return o_sum, g_sum


def ffn_keep_kernel(half, bits, n3, e3, o_in, g_in, w_in, b_in, w_out,
                    du, part_own, part_par, pdn, f_out, b_grad, acc):
    i = pl.program_id(0)
    o, g = ffn_half(i, n3[...], e3[...], w_in, b_in, w_out, du, f_out, b_grad, acc)
    pdn[...] = (g + g_in[...].astype(F32)).astype(BF16)
    o = (o + o_in[...].astype(F32)).astype(BF16)

    @pl.when(i < half)
    def _():
        part_own[...] = o

    @pl.when(i >= half)
    def _():
        part_par[...] = o


def ffn_in_kernel(bits, n3, du_a, du_b, send, keep):
    n = n3[...]
    other = pl.program_id(1) != bits[0]

    @pl.when(pl.program_id(0) == 0)
    def _():
        @pl.when(other)
        def _():
            send[...] = dot_tn(n, du_a[...]).astype(BF16)

        @pl.when(jnp.logical_not(other))
        def _():
            send[...] = dot_tn(n, du_b[...]).astype(BF16)

    @pl.when(pl.program_id(0) == 1)
    def _():
        @pl.when(other)
        def _():
            keep[...] = dot_tn(n, du_a[...]).astype(BF16)

        @pl.when(jnp.logical_not(other))
        def _():
            keep[...] = dot_tn(n, du_b[...]).astype(BF16)


def cross_bwd_kernel(rows, length, heads, half, pick, h2, part, recv, eo, ep, gains, wo, c2, p, kv, wq, a2, n2,
                     dh2, dkv, pdn, sums, sums_in, g_out, g_q, dk_acc, dv_acc, dk_row, dv_row, dq_buf,
                     out_acc, q_acc):
    i = pl.program_id(0)
    width = heads * HEAD

    @pl.when(i == 0)
    def _():
        sums[...] = jnp.zeros_like(sums)
        sums_in[...] = jnp.zeros_like(sums_in)
        dk_acc[...] = jnp.zeros_like(dk_acc)
        dv_acc[...] = jnp.zeros_like(dv_acc)
        out_acc[...] = jnp.zeros_like(out_acc)
        q_acc[...] = jnp.zeros_like(q_acc)

    dn = part[...].astype(F32) + recv[...].astype(F32)
    y, rs = norm_parts(h2[...])
    g3 = jnp.where(i < half, eo[...].astype(F32), ep[...].astype(F32))
    d = g3 + norm_back(dn, y, rs, gains[2:3, :].astype(F32))
    dh2[...] = d
    e = d.astype(BF16)

    @pl.when(i < half)
    def _():
        sums[0:1, :] += jnp.sum(dn * y, axis=0, keepdims=True)
        sums[1:2, :] += jnp.sum(dn, axis=0, keepdims=True)
        sums[2:3, :] += jnp.sum(d, axis=0, keepdims=True)
        sums[3:4, :] += jnp.sum(g3, axis=0, keepdims=True)

    da = dot_nt(e, wo[...]).astype(BF16).astype(F32)
    cf = c2[...].astype(F32)
    for r in range(rows):
        at = slice(r * length, (r + 1) * length)
        im = pick[i * rows + r]
        kr = kv[im, :, 0:width]
        vr = kv[im, :, width : 2 * width]
        pr = p[r]
        wide_o = spread_heads(da[at], heads)
        dpt = dot_nt(vr, wide_o)
        dv_row[r] = dot_nn(pr, wide_o)
        pf = pr.astype(F32)
        ds = (pf * (dpt - jnp.sum(pf * dpt, axis=0, keepdims=True))).astype(BF16)
        dq_buf[at, :] = join_heads(dot_tn(ds, kr), length, heads)
        dk_row[r] = dot_nn(ds, spread_heads(cf[at], heads))
    dc = (dq_buf[...] * SCALE).astype(BF16)
    pdn[...] = dot_nt(dc, wq[...]).astype(BF16)
    sums_in[0:1, :] += jnp.sum(dc.astype(F32), axis=0, keepdims=True)
    out_acc[...] += dot_tn(a2[...], e)
    q_acc[...] += dot_tn(n2[...], dc)
    for r in range(rows):
        im = pick[i * rows + r]
        dk_acc[im] += dk_row[r]
        dv_acc[im] += dv_row[r]

    @pl.when(i == pl.num_programs(0) - 1)
    def _():
        total = None
        for j in range(dkv.shape[0]):
            dkv[j, :, 0:width] = (dk_acc[j] * SCALE).astype(BF16)
            low = dv_acc[j].astype(BF16)
            dkv[j, :, width : 2 * width] = low
            s = jnp.sum(low.astype(F32), axis=0, keepdims=True)
            total = s if total is None else total + s
        sums_in[1:2, :] = total
        g_out[...] = out_acc[...].astype(BF16)
        fold = q_acc.shape[0] // 2
        g_q[:, 0:width] = q_acc[0:fold, :].astype(BF16)
        g_q[:, width : 2 * width] = q_acc[fold : 2 * fold, :].astype(BF16)


def kv_grad_kernel(bits, po, pp, dkv, w_own, w_par, g_out, g_q, send, keep, terms_own, terms_par, own_acc, par_acc,
                   own_cols, par_cols, d_cols):
    i = pl.program_id(0)

    @pl.when(i == 0)
    def _():
        own_acc[...] = jnp.zeros_like(own_acc)
        par_acc[...] = jnp.zeros_like(par_acc)
        own_cols[...] = jnp.zeros_like(own_cols)
        par_cols[...] = jnp.zeros_like(par_cols)
        d_cols[...] = jnp.zeros_like(d_cols)

    spots = po.shape[1]
    pad = own_cols.shape[0] // po.shape[0]
    for j in range(po.shape[0]):
        d = dkv[j]
        at = slice(j * pad, j * pad + spots)
        own_cols[at, :] = po[j]
        par_cols[at, :] = pp[j]
        d_cols[at, :] = d
        terms_own[j] = dot_nt(d, w_own[...]).astype(BF16)
        terms_par[j] = dot_nt(d, w_par[...]).astype(BF16)
    d = d_cols[...]
    own_acc[...] += dot_tn(own_cols[...], d)
    par_acc[...] += dot_tn(par_cols[...], d)

    @pl.when(i == pl.num_programs(0) - 1)
    def _():
        cut = g_out.shape[0]

        @pl.when(bits[0] == 0)
        def _():
            keep[0:cut, :] = g_out[...]
            keep[cut:, :] = own_acc[...].astype(BF16)
            send[0:cut, :] = g_q[...]
            send[cut:, :] = par_acc[...].astype(BF16)

        @pl.when(bits[0] != 0)
        def _():
            send[0:cut, :] = g_out[...]
            send[cut:, :] = own_acc[...].astype(BF16)
            keep[0:cut, :] = g_q[...]
            keep[cut:, :] = par_acc[...].astype(BF16)


def self_bwd_kernel(rows, length, heads, half, bits, h1, dh2, part, recv, xo, xp, gains, wo, q, k, v, p, w, a1, n1,
                    sums2, sums_in2, b_grad_a, b_grad_b,
                    dh1, part_own, part_par, send, keep, q_buf, k_buf, v_buf, out_acc, w_acc, sums, sums_in):
    i = pl.program_id(0)
    width = heads * HEAD

    @pl.when(i == 0)
    def _():
        sums[...] = jnp.zeros_like(sums)
        sums_in[...] = jnp.zeros_like(sums_in)
        out_acc[...] = jnp.zeros_like(out_acc)
        w_acc[...] = jnp.zeros_like(w_acc)

    dn = part[...].astype(F32) + recv[...].astype(F32)
    y, rs = norm_parts(h1[...])
    d = dh2[...] + norm_back(dn, y, rs, gains[1:2, :].astype(F32))
    e = d.astype(BF16)

    @pl.when(i < half)
    def _():
        dh1[...] = d
        sums[2:3, :] += jnp.sum(dn * y, axis=0, keepdims=True)
        sums[3:4, :] += jnp.sum(dn, axis=0, keepdims=True)
        sums[4:5, :] += jnp.sum(d, axis=0, keepdims=True)

    da = dot_nt(e, wo[...]).astype(BF16).astype(F32)
    qf, kf, vf = q[...].astype(F32), k[...].astype(F32), v[...].astype(F32)
    for r in range(rows):
        at = slice(r * length, (r + 1) * length)
        kr = kf[at].astype(BF16)
        vr = vf[at].astype(BF16)
        pr = p[r]
        wide_o = spread_heads(da[at], heads)
        dpt = dot_nt(vr, wide_o)
        v_buf[at, :] = dot_nn(pr, wide_o)
        pf = pr.astype(F32)
        ds = (pf * (dpt - jnp.sum(pf * dpt, axis=0, keepdims=True))).astype(BF16)
        q_buf[at, :] = join_heads(dot_tn(ds, kr), length, heads)
        k_buf[at, :] = dot_nn(ds, spread_heads(qf[at], heads))
    dqv = (q_buf[...] * SCALE).astype(BF16)
    dkv = (k_buf[...] * SCALE).astype(BF16)
    dvv = v_buf[...].astype(BF16)
    sums_in[0:1, :] += jnp.sum(dqv.astype(F32), axis=0, keepdims=True)
    sums_in[1:2, :] += jnp.sum(dvv.astype(F32), axis=0, keepdims=True)
    back = dot_nt(dqv, w[0]) + dot_nt(dkv, w[1]) + dot_nt(dvv, w[2])
    low = back.astype(BF16)

    @pl.when(i < half)
    def _():
        part_own[...] = low

    @pl.when(i >= half)
    def _():
        part_par[...] = low

    x = jnp.where(i < half, xo[...].astype(F32), xp[...].astype(F32))
    y0, _ = norm_parts(x)
    sums[0:1, :] += jnp.sum(back * y0, axis=0, keepdims=True)
    sums[1:2, :] += jnp.sum(back, axis=0, keepdims=True)
    out_acc[...] += dot_tn(a1[...], e)
    n = n1[...]
    w_acc[0] += dot_tn(n, dqv)
    w_acc[1] += dot_tn(n, dkv)
    w_acc[2] += dot_tn(n, dvv)

    @pl.when(i == pl.num_programs(0) - 1)
    def _():
        cut = out_acc.shape[0]
        fold = w_acc.shape[1] // 2
        extra = (send.shape[0] - 2 * cut)

        def folded(ref, base, j):
            ref[base : base + fold, 0:width] = w_acc[j, 0:fold, :].astype(BF16)
            ref[base : base + fold, width : 2 * width] = w_acc[j, fold : 2 * fold, :].astype(BF16)

        def first(ref):
            ref[0:cut, :] = out_acc[...].astype(BF16)
            folded(ref, cut, 0)
            pad = jnp.zeros((extra - 16, 2 * width), F32)
            ref[2 * cut :, :] = jnp.concatenate([sums[0:8, :], sums2[0:8, :], pad], axis=0).astype(BF16)

        def second(ref):
            folded(ref, 0, 1)
            folded(ref, fold, 2)
            rows_in = jnp.concatenate([sums_in[0:8, :], sums_in2[0:8, :]], axis=0)
            left = jnp.concatenate([rows_in, jnp.zeros_like(rows_in)], axis=1)
            low, high = jnp.where(bits[2] == 0, b_grad_b[...], b_grad_a[...]), jnp.where(
                bits[2] == 0, b_grad_a[...], b_grad_b[...])
            bias_rows = jnp.concatenate(
                [low, high, jnp.zeros((extra - 18, 2 * width), F32)], axis=0)
            ref[2 * fold :, :] = jnp.concatenate([left, bias_rows], axis=0).astype(BF16)

        @pl.when(bits[0] == 0)
        def _():
            first(keep)
            second(send)

        @pl.when(bits[0] != 0)
        def _():
            first(send)
            second(keep)


def text_bwd_kernel(x, dh1, part, recv, gains, out):
    dn = part[...].astype(F32) + recv[...].astype(F32)
    y, rs = norm_parts(x[...].astype(F32))
    out[...] = dh1[...] + norm_back(dn, y, rs, gains[0:1, :].astype(F32))


def widen_kernel(bits, mine, got, out):
    out[...] = jnp.where(pl.program_id(0) == bits[0], mine[...].astype(F32), got[...].astype(F32))


def open_cross_kernel(cut, bits, mine, got, g_out, g_q, g_kv):
    width = g_q.shape[1]
    zero = bits[0] == 0
    core = bits[1]
    deep = mine.shape[0] - cut
    g_out[...] = jnp.where(zero, mine[0:cut, :].astype(F32), got[0:cut, :].astype(F32))
    q = jnp.where(zero, got[0:cut, :].astype(F32), mine[0:cut, :].astype(F32))
    fold = q.shape[0]
    g_q[0:fold, :] = q[:, 0:width]
    g_q[fold : 2 * fold, :] = q[:, width : 2 * width]
    swapped = jnp.logical_xor(zero, core == 0)
    g_kv[0:deep, :] = jnp.where(swapped, got[cut:, :].astype(F32), mine[cut:, :].astype(F32))
    g_kv[deep : 2 * deep, :] = jnp.where(swapped, mine[cut:, :].astype(F32), got[cut:, :].astype(F32))


def open_self_kernel(cut, fold, bits, mine, got, g_out, g_w, rows_a, rows_in, rows_ffn):
    zero = bits[0] == 0
    width = g_w.shape[2]

    def first(at):
        return jnp.where(zero, mine[at, :].astype(F32), got[at, :].astype(F32))

    def second(at):
        return jnp.where(zero, got[at, :].astype(F32), mine[at, :].astype(F32))

    def unfold(j, v):
        g_w[j, 0:fold, :] = v[:, 0:width]
        g_w[j, fold : 2 * fold, :] = v[:, width : 2 * width]

    g_out[...] = first(slice(0, cut))
    unfold(0, first(slice(cut, cut + fold)))
    unfold(1, second(slice(0, fold)))
    unfold(2, second(slice(fold, 2 * fold)))
    r = first(slice(2 * cut, 2 * cut + 16))
    rows_a[...] = jnp.concatenate([r[0:1], r[2:3], r[8:9], r[1:2], r[3:4], r[9:10], r[4:5], r[10:12], r[0:7]], axis=0)
    r = second(slice(2 * fold, 2 * fold + 32))
    rows_in[...] = jnp.concatenate([r[0:2, 0:width], r[8:10, 0:width]], axis=0)
    rows_ffn[...] = r[16:18]


def whole(shape):
    zeros = (0,) * len(shape)
    return pl.BlockSpec(shape, lambda *_: zeros)


def call(kernel, name, grid, ins, outs, args, scratch=(), prefetch=0, flops=0, exps=0):
    moved = sum(a.size * a.dtype.itemsize for a in args) + sum(
        functools.reduce(lambda u, v: u * v, s.shape, 1) * s.dtype.itemsize for s, _ in outs
    )
    return pl.pallas_call(
        kernel,
        out_shape=[s for s, _ in outs],
        grid_spec=pltpu.PrefetchScalarGridSpec(
            num_scalar_prefetch=prefetch,
            grid=grid,
            in_specs=list(ins),
            out_specs=[b for _, b in outs],
            scratch_shapes=list(scratch),
        ),
        compiler_params=pltpu.CompilerParams(vmem_limit_bytes=VMEM_BYTES),
        cost_estimate=pl.CostEstimate(flops=flops, transcendentals=exps, bytes_accessed=moved),
        name=name,
    )(*args)


def local(n_dp, plans, text, patches, segment_ids, image_of_row, gains, shifts, self_qkv, in_bias, self_out,
          cross_q, cross_kv, cross_out, ffn_in, ffn_in_bias, ffn_out, out_bias, cotangent):
    core = lax.axis_index("tensor")
    dp = lax.axis_index("dp")
    own, width = text.shape
    tokens = 2 * own
    rows, length = segment_ids.shape
    local_width = self_out.shape[0]
    heads = local_width // HEAD
    images, spots, half_dv = patches.shape
    hidden = ffn_in.shape[1]
    wide = hidden // 2
    block_rows = rows // 2
    block = block_rows * length
    steps = tokens // block
    half = steps // 2
    sd = jax.ShapeDtypeStruct

    swap = lambda v: lax.ppermute(v, "tensor", [(0, 1), (1, 0)])
    text_par = swap(text)
    cot_par = swap(cotangent)
    patches_par = swap(patches)

    def bit_of(level):
        return jnp.where(core == 0, dp >> level[0], dp >> level[1]) & 1

    def send_along(value, level):
        perm = [(d * 2 + t, (d ^ (1 << level[t])) * 2 + t) for d in range(n_dp) for t in range(2)]
        return lax.ppermute(value, ("dp", "tensor"), perm)

    def add(a, b):
        return (a.astype(F32) + b.astype(F32)).astype(BF16)

    def after(value, *others):
        return lax.optimization_barrier((value,) + others)[0]

    def reduce_chain(send, keep, plan):
        halving, doubling = plan
        got = yield send, halving[0]
        keep = keep()
        for level in halving[1:]:
            n = keep.shape[0] // 2
            bit = bit_of(level)
            cut = lambda v, b: lax.dynamic_slice_in_dim(v, b * n, n, axis=0)
            send = add(cut(keep, 1 - bit), cut(got, 1 - bit))
            keep = add(cut(keep, bit), cut(got, bit))
            got = yield send, level
        value = add(keep, got)
        for level in doubling:
            got = yield value, level
            value = add(value, got)
        for level in reversed(halving[1:]):
            got = yield value, level
            place = lax.broadcasted_iota(jnp.int32, (2,) + value.shape, 0)
            value = jnp.where(place == bit_of(level), value[None], got[None]).reshape(-1, value.shape[1])
        got = yield value, halving[0]
        return value, got

    class Chain:
        def __init__(self, send, keep, plan):
            self.steps = reduce_chain(send, keep, plan)
            self.result = None
            self.sent, self.level = next(self.steps)

        def launch(self):
            self.got = send_along(self.sent, self.level)

        def advance(self, *hold):
            got = after(self.got, *hold) if hold else self.got
            try:
                self.sent, self.level = self.steps.send(got)
            except StopIteration as stop:
                self.result = stop.value

    def fence(chains, gate, *done):
        values = lax.optimization_barrier(tuple(c.sent for c in chains) + (gate,) + done)
        for c, v in zip(chains, values):
            c.sent = v
            c.launch()
        return values[len(chains)]

    first_bits = [
        jnp.stack([bit_of(plan[0][0]), core, bit_of(plans[0][0][0])]).astype(jnp.int32) for plan in plans]
    bits_out, bits_in, bits_cross, bits_self = first_bits

    w3 = jnp.transpose(self_qkv, (1, 0, 2))
    wkv = cross_kv.reshape(cross_kv.shape[0], 2 * local_width)
    flip = lambda v: jnp.where(core == 0, v, jnp.roll(v, rows // 2, axis=0))
    seg = flip(segment_ids)
    pick = flip(image_of_row)
    segk = seg[:, :, None]
    segq = jnp.tile(seg, (1, heads))[:, None, :]

    tok = lambda n: pl.BlockSpec((block, n), lambda i, *_: (i, 0))
    tok_other = lambda n: pl.BlockSpec((block, n), lambda i, *_: ((i + half) % steps, 0))
    tok_own = lambda n: pl.BlockSpec((block, n), lambda i, *_: (jnp.minimum(i, half - 1), 0))
    tok_par = lambda n: pl.BlockSpec((block, n), lambda i, *_: (jnp.maximum(i - half, 0), 0))
    row3 = lambda a, b: pl.BlockSpec((block_rows, a, b), lambda i, *_: (i, 0, 0))
    act = lambda n, dt=BF16: (sd((tokens, n), dt), tok(n))
    full = lambda shape, dt=BF16: (sd(shape, dt), whole(shape))
    ql = heads * length
    sizes = (block_rows, length, heads, half)

    n1, q, k, v, p1, a1, part1 = call(
        functools.partial(self_fwd_kernel, *sizes), "self_fwd", (steps,),
        [tok_own(width), tok_par(width), whole(gains.shape), whole(shifts.shape), whole(w3.shape),
         whole(in_bias.shape), whole(self_out.shape), row3(length, 1), row3(1, ql)],
        [act(width), act(local_width), act(local_width), act(local_width),
         (sd((rows, length, ql), BF16), row3(length, ql)), act(local_width), act(width)],
        (text, text_par, gains, shifts, w3, in_bias, self_out, segk, segq),
        flops=2 * tokens * width * 4 * local_width, exps=rows * length * ql)
    recv1 = swap(part1)

    kv_bias = jnp.concatenate([jnp.zeros((local_width,), F32), in_bias[3].astype(F32)])[None, :]
    place = jnp.full((1,), core, jnp.int32)
    group = 3 if images % 3 == 0 else 1
    image_block = lambda n: pl.BlockSpec((group, spots, n), lambda i, *_: (i, 0, 0))
    (kv,) = call(
        project_kernel, "project", (images // group,),
        [image_block(half_dv), image_block(half_dv),
         pl.BlockSpec((half_dv, 2 * local_width), lambda i, c: (c[0], 0)),
         pl.BlockSpec((half_dv, 2 * local_width), lambda i, c: (1 - c[0], 0)),
         whole(kv_bias.shape)],
        [(sd((images, spots, 2 * local_width), BF16), image_block(2 * local_width))],
        (place, patches, patches_par, wkv, wkv, kv_bias), prefetch=1,
        flops=4 * images * spots * 2 * half_dv * local_width)

    h1, n2, c2, p2, a2, part2 = call(
        functools.partial(cross_fwd_kernel, *sizes), "cross_fwd", (steps,),
        [tok_own(width), tok_par(width), tok(width), tok_other(width), whole(gains.shape), whole(shifts.shape),
         whole(in_bias.shape), whole(out_bias.shape), whole(cross_q.shape), whole(kv.shape), whole(cross_out.shape)],
        [act(width, F32), act(width), act(local_width), (sd((rows, spots, ql), BF16), row3(spots, ql)),
         act(local_width), act(width)],
        (pick, text, text_par, part1, recv1, gains, shifts, in_bias, out_bias, cross_q, kv, cross_out), prefetch=1,
        flops=2 * tokens * width * 2 * local_width + 4 * rows * ql * spots * local_width, exps=rows * ql * spots)
    recv2 = swap(part2)

    own_spec = lambda n: (sd((own, n), BF16), tok_own(n))
    par_spec = lambda n: (sd((own, n), BF16), tok_par(n))
    b_in = ffn_in_bias[None, :]
    half_specs = lambda at: [
        pl.BlockSpec((width, wide), lambda i, b: (0, at(b[0]))),
        pl.BlockSpec((1, wide), lambda i, b: (0, at(b[0]))),
        pl.BlockSpec((wide, width), lambda i, b: (at(b[0]), 0))]
    ffn_acc = [pltpu.VMEM((wide, width), F32)]
    ffn_cost = dict(flops=5 * tokens * width * hidden, exps=tokens * hidden)
    h2, n3, e3, du_a, o_sum, g_sum, out_send, b_grad_a = call(
        functools.partial(ffn_send_kernel, half), "ffn_send", (steps,),
        [tok(width), tok(width), tok_other(width), tok_own(width), tok_par(width), whole(gains.shape),
         whole(shifts.shape), whole(out_bias.shape)] + half_specs(lambda b: 1 - b),
        [act(width, F32), act(width), act(width), act(wide), act(width), act(width), full((wide, width)),
         full((1, wide), F32)],
        (bits_out, h1, part2, recv2, cotangent, cot_par, gains, shifts, out_bias, ffn_in, b_in, ffn_out),
        scratch=ffn_acc, prefetch=1, **ffn_cost)
    chain_out = Chain(out_send, lambda: out_keep, plans[0])
    gate = fence([chain_out], bits_out)
    du_b, part3_own, part3_par, pdn3, out_keep, b_grad_b = call(
        functools.partial(ffn_keep_kernel, half), "ffn_keep", (steps,),
        [tok(width), tok(width), tok(width), tok(width)] + half_specs(lambda b: b),
        [act(wide), own_spec(width), par_spec(width), act(width), full((wide, width)), full((1, wide), F32)],
        (gate, n3, e3, o_sum, g_sum, ffn_in, b_in, ffn_out),
        scratch=ffn_acc, prefetch=1, **ffn_cost)
    recv3 = swap(pdn3)
    chain_out.advance()
    recv_out = swap(part3_par)
    layer_out = h2[:own] + (part3_own.astype(F32) + recv_out.astype(F32)) + out_bias[2].astype(F32)

    hw = width // 2
    gate = fence([chain_out], jnp.stack([bits_out[0], bits_in[0]]), pdn3)
    in_send, in_keep = call(
        ffn_in_kernel, "ffn_in_grad", (2, 2),
        [pl.BlockSpec((tokens, hw), lambda j, c, b: (0, jnp.where(j == 0, 1 - b[1], b[1]))),
         whole((tokens, wide)), whole((tokens, wide))],
        [(sd((width, wide), BF16), pl.BlockSpec((hw, wide), lambda j, c, b: (jnp.where(j == 0, c, 1), 0))),
         (sd((width, wide), BF16), pl.BlockSpec((hw, wide), lambda j, c, b: (jnp.where(j == 0, 0, c), 0)))],
        (gate, n3, du_a, du_b), prefetch=1, flops=2 * tokens * width * hidden)

    chain_in = Chain(in_send, lambda: in_keep, plans[1])
    chain_out.advance()
    gate = fence([chain_out, chain_in], pick)
    dh2, dkv, pdn2, sums2, sums_in2, g_cross_out, g_cross_q = call(
        functools.partial(cross_bwd_kernel, *sizes), "cross_bwd", (steps,),
        [tok(width), tok(width), tok_other(width), tok_own(width), tok_par(width), whole(gains.shape),
         whole(cross_out.shape), tok(local_width), row3(spots, ql), whole(kv.shape), whole(cross_q.shape),
         tok(local_width), tok(width)],
        [act(width, F32), full(kv.shape), act(width), full((8, width), F32), full((8, local_width), F32),
         full((local_width, width)), full((hw, width))],
        (gate, h2, pdn3, recv3, cotangent, cot_par, gains, cross_out, c2, p2, kv, cross_q, a2, n2), prefetch=1,
        scratch=[pltpu.VMEM((images, spots, local_width), F32)] * 2
        + [pltpu.VMEM((block_rows, spots, local_width), F32)] * 2
        + [pltpu.VMEM((block, local_width), F32), pltpu.VMEM((local_width, width), F32),
           pltpu.VMEM((width, local_width), F32)],
        flops=2 * tokens * width * 4 * local_width + 8 * rows * ql * spots * local_width)
    recv_dn2 = swap(pdn2)
    chain_out.advance()
    chain_in.advance()
    gate = fence([chain_out, chain_in], bits_cross, pdn2)

    deep = local_width + half_dv
    slots = -(-spots // 16) * 16
    cross_send, cross_keep, terms_own, terms_par = call(
        kv_grad_kernel, "kv_grad", (images // group,),
        [image_block(half_dv), image_block(half_dv), image_block(2 * local_width),
         pl.BlockSpec((half_dv, 2 * local_width), lambda i, c: (c[1], 0)),
         pl.BlockSpec((half_dv, 2 * local_width), lambda i, c: (1 - c[1], 0)),
         whole(g_cross_out.shape), whole(g_cross_q.shape)],
        [full((deep, width)), full((deep, width)),
         (sd(patches.shape, BF16), image_block(half_dv)), (sd(patches.shape, BF16), image_block(half_dv))],
        (gate, patches, patches_par, dkv, wkv, wkv, g_cross_out, g_cross_q), prefetch=1,
        scratch=[pltpu.VMEM((half_dv, width), F32)] * 2
        + [pltpu.VMEM((group * slots, half_dv), BF16)] * 2 + [pltpu.VMEM((group * slots, 2 * local_width), BF16)],
        flops=8 * images * spots * 2 * half_dv * local_width)
    chain_cross = Chain(cross_send, lambda: cross_keep, plans[2])
    chain_out.advance()
    chain_in.advance()
    gate = fence([chain_out, chain_in, chain_cross], bits_self)
    patch_grad = terms_own.astype(F32) + swap(terms_par).astype(F32)

    extra = 32
    tall = 2 * local_width + extra
    dh1, part1_own, part1_par, self_send, self_keep = call(
        functools.partial(self_bwd_kernel, *sizes), "self_bwd", (steps,),
        [tok(width), tok(width), tok(width), tok_other(width), tok_own(width), tok_par(width), whole(gains.shape),
         whole(self_out.shape), tok(local_width), tok(local_width), tok(local_width), row3(length, ql),
         whole(w3.shape), tok(local_width), tok(width), whole((8, width)), whole((8, local_width)),
         whole((1, wide)), whole((1, wide))],
        [(sd((own, width), F32), tok_own(width)), own_spec(width), par_spec(width), full((tall, width)),
         full((tall, width))],
        (gate, h1, dh2, pdn2, recv_dn2, text, text_par, gains, self_out, q, k, v, p1, w3, a1, n1, sums2,
         sums_in2, b_grad_a, b_grad_b), prefetch=1,
        scratch=[pltpu.VMEM((block, local_width), F32)] * 3
        + [pltpu.VMEM((local_width, width), F32), pltpu.VMEM((3, width, local_width), F32),
           pltpu.VMEM((8, width), F32), pltpu.VMEM((8, local_width), F32)],
        flops=2 * tokens * width * 8 * local_width)
    recv_dn1 = swap(part1_par)
    chain_self = Chain(self_send, lambda: self_keep, plans[3])
    chain_out.advance()
    chain_in.advance()
    chain_cross.advance()
    last = fence([chain_cross, chain_in, chain_out, chain_self], part1_own)
    text_block = own // 2
    half_block = pl.BlockSpec((text_block, width), lambda i, *_: (i, 0))
    (text_grad,) = call(
        text_bwd_kernel, "text_bwd", (2,),
        [half_block, half_block, half_block, half_block, whole(gains.shape)],
        [(sd((own, width), F32), half_block)],
        (text, dh1, part1_own, recv_dn1, gains))

    piece = pl.BlockSpec((hw, width), lambda j, c, b: (c, 0))
    open_cross = lambda r: (r[2].reshape(cross_kv.shape), r[0], r[1])
    opens = {
        chain_out: lambda got: call(
            widen_kernel, "open_ffn_out", (2, wide // hw), [piece, piece],
            [(sd((hidden, width), F32), pl.BlockSpec((hw, width), lambda j, c, b: (j * (wide // hw) + c, 0)))],
            (bits_out,) + got, prefetch=1),
        chain_in: lambda got: call(
            widen_kernel, "open_ffn_in", (2, 2), [piece, piece],
            [(sd((width, hidden), F32), pl.BlockSpec((hw, wide), lambda j, c, b: (j, c)))],
            (bits_in,) + got, prefetch=1),
        chain_cross: lambda got: open_cross(call(
            functools.partial(open_cross_kernel, local_width), "open_cross", (1,),
            [whole((deep, width)), whole((deep, width))],
            [full((local_width, width), F32), full((width, local_width), F32), full((2 * half_dv, width), F32)],
            (bits_cross,) + got, prefetch=1)),
        chain_self: lambda got: call(
            functools.partial(open_self_kernel, local_width, hw), "open_self", (1,),
            [whole((tall, width)), whole((tall, width))],
            [full((local_width, width), F32), full((3, width, local_width), F32), full((16, width), F32),
             full((4, local_width), F32), full((2, wide), F32)],
            (bits_self,) + got, prefetch=1),
    }
    o, i, c, s = chain_out, chain_in, chain_cross, chain_self
    opened = {}
    order = [c, i, c, s, i, s, o, c, i, s, c, s, c, s, o, s, c, s, i]
    while len(opened) < len(opens):
        chain = order.pop(0) if order else next(v for v in opens if v not in opened)
        if chain in opened:
            continue
        chain.advance(last)
        if chain.result is None:
            chain.launch()
            last = chain.sent
        else:
            opened[chain] = opens[chain](chain.result)
            last = opened[chain][0]
    (ffn_out_grad,), (ffn_in_grad,) = opened[o], opened[i]
    cross_kv_grad, cross_out_grad, cross_q_grad = opened[c]
    self_out_grad, qkv_grad, rows_a, in_bias_grad, rows_ffn = opened[s]
    self_qkv_grad = jnp.transpose(qkv_grad, (1, 0, 2))

    rows_a = rows_a + swap(rows_a)
    gains_grad, shifts_grad, out_bias_grad = rows_a[0:3], rows_a[3:6], rows_a[6:9]
    ffn_in_bias_grad = rows_ffn.reshape(hidden)

    return (layer_out, text_grad, patch_grad, gains_grad, shifts_grad, self_qkv_grad, in_bias_grad, self_out_grad,
            cross_q_grad, cross_kv_grad, cross_out_grad, ffn_in_grad, ffn_in_bias_grad, ffn_out_grad, out_bias_grad)


def make_plans(mesh):
    bits = mesh.shape["dp"].bit_length() - 1
    third = (bits + 1) // 4
    x, y, z = list(range(third)), list(range(third, 2 * third)), list(range(2 * third, bits))
    flat = list(zip(x + y, y + x))
    up = list(zip(z, z))
    return [(flat + up[:1], up[1:])] * 4


def solution(mesh):
    both = P(("dp", "tensor"), None)
    in_specs = (both, P("dp", None, "tensor"), P("dp", None), P("dp"), P(), P(), P(None, None, "tensor"),
                P(None, "tensor"), P("tensor", None), P(None, "tensor"), P(None, None, "tensor"), P("tensor", None),
                P(None, "tensor"), P("tensor"), P("tensor", None), P(), both)
    out_specs = (both, both, P("dp", None, "tensor"), P(), P(), P(None, None, "tensor"), P(None, "tensor"),
                 P("tensor", None), P(None, "tensor"), P(None, None, "tensor"), P("tensor", None), P(None, "tensor"),
                 P("tensor"), P("tensor", None), P())
    fn = functools.partial(local, mesh.shape["dp"], make_plans(mesh))
    return jax.shard_map(fn, mesh=mesh, in_specs=in_specs, out_specs=out_specs, check_vma=False)
```

```python
import functools

import jax
import jax.numpy as jnp
from jax import lax
from jax.experimental import pallas as pl
from jax.experimental.pallas import tpu as pltpu
from jax.sharding import PartitionSpec as P

HEAD = 64
EPSILON = 1e-06
SCALE = 0.125
NEGATIVE = -1000000000.0
F32 = jnp.float32
BF16 = jnp.bfloat16
VMEM_BYTES = 60 * 1024 * 1024


def dot_nn(a, b):
    return lax.dot_general(a, b, (((1,), (0,)), ((), ())), preferred_element_type=F32)


def dot_nt(a, b):
    return lax.dot_general(a, b, (((1,), (1,)), ((), ())), preferred_element_type=F32)


def dot_tn(a, b):
    return lax.dot_general(a, b, (((0,), (0,)), ((), ())), preferred_element_type=F32)


def norm_parts(v):
    centre = v - jnp.mean(v, axis=-1, keepdims=True)
    spread = jnp.mean(centre * centre, axis=-1, keepdims=True)
    r = lax.rsqrt(spread + EPSILON)
    return centre * r, r


def norm_back(dn, y, r, gain):
    w = dn * gain
    return r * (w - jnp.mean(w, axis=-1, keepdims=True) - y * jnp.mean(w * y, axis=-1, keepdims=True))


def spread_heads(row, heads):
    column = lax.broadcasted_iota(jnp.int32, row.shape, 1) // HEAD
    return jnp.concatenate(
        [jnp.where(column == h, row, 0.0) for h in range(heads)], axis=0
    ).astype(BF16)


def join_heads(wide, length, heads):
    column = lax.broadcasted_iota(jnp.int32, (length, heads * HEAD), 1) // HEAD
    out = wide[0:length]
    for h in range(1, heads):
        out = jnp.where(column == h, wide[h * length : (h + 1) * length], out)
    return out


def softmax_columns(st):
    top = jnp.max(st, axis=0, keepdims=True)
    e = jnp.exp(st - top)
    return e / jnp.sum(e, axis=0, keepdims=True)


def self_fwd_kernel(rows, length, heads, half, xo, xp, gains, shifts, w, bias, wo, segk, segq,
                    n1, q, k, v, p, a, part):
    i = pl.program_id(0)
    x = jnp.where(i < half, xo[...].astype(F32), xp[...].astype(F32))
    y, _ = norm_parts(x)
    n = (y * gains[0:1, :].astype(F32) + shifts[0:1, :].astype(F32)).astype(BF16)
    n1[...] = n
    b = bias[...].astype(F32)
    qv = (dot_nn(n, w[0]) + b[0:1]).astype(BF16)
    kv = dot_nn(n, w[1]).astype(BF16)
    vv = (dot_nn(n, w[2]) + b[1:2]).astype(BF16)
    q[...] = qv
    k[...] = kv
    v[...] = vv
    qf, kf, vf = qv.astype(F32), kv.astype(F32), vv.astype(F32)
    outs = []
    for r in range(rows):
        at = slice(r * length, (r + 1) * length)
        kr = kf[at].astype(BF16)
        vr = vf[at].astype(BF16)
        st = dot_nt(kr, spread_heads(qf[at], heads)) * SCALE
        st = jnp.where(segk[r] == segq[r], st, NEGATIVE)
        pr = softmax_columns(st).astype(BF16)
        p[r] = pr
        outs.append(join_heads(dot_tn(pr, vr), length, heads))
    av = jnp.concatenate(outs, axis=0).astype(BF16)
    a[...] = av
    part[...] = dot_nn(av, wo[...]).astype(BF16)


def project_kernel(place, po, pp, w0, w1, bias, kv):
    for j in range(po.shape[0]):
        x = dot_nn(po[j], w0[...]) + dot_nn(pp[j], w1[...])
        kv[j] = (x + bias[...]).astype(BF16)


def cross_fwd_kernel(rows, length, heads, half, pick, xo, xp, part, recv, gains, shifts, bias, out_bias,
                     wq, kv, wo, h1, n2, c2, p, a, part2):
    i = pl.program_id(0)
    x = jnp.where(i < half, xo[...].astype(F32), xp[...].astype(F32))
    h = x + (part[...].astype(F32) + recv[...].astype(F32)) + out_bias[0:1, :].astype(F32)
    h1[...] = h
    y, _ = norm_parts(h)
    n = (y * gains[1:2, :].astype(F32) + shifts[1:2, :].astype(F32)).astype(BF16)
    n2[...] = n
    cv = (dot_nn(n, wq[...]) + bias[2:3, :].astype(F32)).astype(BF16)
    c2[...] = cv
    cf = cv.astype(F32)
    width = heads * HEAD
    outs = []
    for r in range(rows):
        at = slice(r * length, (r + 1) * length)
        im = pick[i * rows + r]
        kr = kv[im, :, 0:width]
        vr = kv[im, :, width : 2 * width]
        st = dot_nt(kr, spread_heads(cf[at], heads)) * SCALE
        pr = softmax_columns(st).astype(BF16)
        p[r] = pr
        outs.append(join_heads(dot_tn(pr, vr), length, heads))
    av = jnp.concatenate(outs, axis=0).astype(BF16)
    a[...] = av
    part2[...] = dot_nn(av, wo[...]).astype(BF16)


def ffn_send_kernel(half, bits, h1, part, recv, eo, ep, gains, shifts, out_bias, w_in, b_in, w_out,
                    h2, n3, e3, du, o_sum, g_sum, f_out, b_grad, acc):
    i = pl.program_id(0)
    h = h1[...] + (part[...].astype(F32) + recv[...].astype(F32)) + out_bias[1:2, :].astype(F32)
    h2[...] = h
    y, _ = norm_parts(h)
    n = (y * gains[2:3, :].astype(F32) + shifts[2:3, :].astype(F32)).astype(BF16)
    n3[...] = n
    e = jnp.where(i < half, eo[...].astype(F32), ep[...].astype(F32)).astype(BF16)
    e3[...] = e
    o, g = ffn_half(i, n, e, w_in, b_in, w_out, du, f_out, b_grad, acc)
    o_sum[...] = o.astype(BF16)
    g_sum[...] = g.astype(BF16)


def ffn_half(i, n, e, w_in, b_in, w_out, du, f_out, b_grad, acc):
    chunk = 384 if w_in.shape[1] % 384 == 0 else w_in.shape[1]
    last = i == pl.num_programs(0) - 1

    @pl.when(i == 0)
    def _():
        b_grad[...] = jnp.zeros_like(b_grad)
        acc[...] = jnp.zeros_like(acc)

    o_sum, g_sum = None, None
    for c in range(w_in.shape[1] // chunk):
        at = slice(c * chunk, (c + 1) * chunk)
        u = dot_nn(n, w_in[:, at]) + b_in[:, at].astype(F32)
        cdf = 0.5 * (1.0 + lax.erf(u * 0.7071067811865476))
        m = (u * cdf).astype(BF16)
        slope = cdf + u * (jnp.exp(-0.5 * u * u) * 0.3989422804014327)
        d = (dot_nt(e, w_out[at, :]) * slope).astype(BF16)
        du[:, at] = d
        b_grad[:, at] += jnp.sum(d.astype(F32), axis=0, keepdims=True)
        o = dot_nn(m, w_out[at, :])
        g = dot_nt(d, w_in[:, at])
        o_sum = o if o_sum is None else o_sum + o
        g_sum = g if g_sum is None else g_sum + g
        acc[at, :] += dot_tn(m, e)

    @pl.when(last)
    def _():
        f_out[...] = acc[...].astype(BF16)

    return o_sum, g_sum


def ffn_keep_kernel(half, bits, n3, e3, o_in, g_in, w_in, b_in, w_out,
                    du, part_own, part_par, pdn, f_out, b_grad, acc):
    i = pl.program_id(0)
    o, g = ffn_half(i, n3[...], e3[...], w_in, b_in, w_out, du, f_out, b_grad, acc)
    pdn[...] = (g + g_in[...].astype(F32)).astype(BF16)
    o = (o + o_in[...].astype(F32)).astype(BF16)

    @pl.when(i < half)
    def _():
        part_own[...] = o

    @pl.when(i >= half)
    def _():
        part_par[...] = o


def ffn_in_kernel(bits, n3, du_a, du_b, send, keep):
    n = n3[...]
    other = pl.program_id(1) != bits[0]

    @pl.when(pl.program_id(0) == 0)
    def _():
        @pl.when(other)
        def _():
            send[...] = dot_tn(n, du_a[...]).astype(BF16)

        @pl.when(jnp.logical_not(other))
        def _():
            send[...] = dot_tn(n, du_b[...]).astype(BF16)

    @pl.when(pl.program_id(0) == 1)
    def _():
        @pl.when(other)
        def _():
            keep[...] = dot_tn(n, du_a[...]).astype(BF16)

        @pl.when(jnp.logical_not(other))
        def _():
            keep[...] = dot_tn(n, du_b[...]).astype(BF16)


def cross_bwd_kernel(rows, length, heads, half, pick, h2, part, recv, eo, ep, gains, wo, c2, p, kv, wq, a2, n2,
                     dh2, dkv, pdn, sums, sums_in, g_out, g_q, dk_acc, dv_acc, dk_row, dv_row, dq_buf,
                     out_acc, q_acc):
    i = pl.program_id(0)
    width = heads * HEAD

    @pl.when(i == 0)
    def _():
        sums[...] = jnp.zeros_like(sums)
        sums_in[...] = jnp.zeros_like(sums_in)
        dk_acc[...] = jnp.zeros_like(dk_acc)
        dv_acc[...] = jnp.zeros_like(dv_acc)
        out_acc[...] = jnp.zeros_like(out_acc)
        q_acc[...] = jnp.zeros_like(q_acc)

    dn = part[...].astype(F32) + recv[...].astype(F32)
    y, rs = norm_parts(h2[...])
    g3 = jnp.where(i < half, eo[...].astype(F32), ep[...].astype(F32))
    d = g3 + norm_back(dn, y, rs, gains[2:3, :].astype(F32))
    dh2[...] = d
    e = d.astype(BF16)

    @pl.when(i < half)
    def _():
        sums[0:1, :] += jnp.sum(dn * y, axis=0, keepdims=True)
        sums[1:2, :] += jnp.sum(dn, axis=0, keepdims=True)
        sums[2:3, :] += jnp.sum(d, axis=0, keepdims=True)
        sums[3:4, :] += jnp.sum(g3, axis=0, keepdims=True)

    da = dot_nt(e, wo[...]).astype(BF16).astype(F32)
    cf = c2[...].astype(F32)
    for r in range(rows):
        at = slice(r * length, (r + 1) * length)
        im = pick[i * rows + r]
        kr = kv[im, :, 0:width]
        vr = kv[im, :, width : 2 * width]
        pr = p[r]
        wide_o = spread_heads(da[at], heads)
        dpt = dot_nt(vr, wide_o)
        dv_row[r] = dot_nn(pr, wide_o)
        pf = pr.astype(F32)
        ds = (pf * (dpt - jnp.sum(pf * dpt, axis=0, keepdims=True))).astype(BF16)
        dq_buf[at, :] = join_heads(dot_tn(ds, kr), length, heads)
        dk_row[r] = dot_nn(ds, spread_heads(cf[at], heads))
    dc = (dq_buf[...] * SCALE).astype(BF16)
    pdn[...] = dot_nt(dc, wq[...]).astype(BF16)
    sums_in[0:1, :] += jnp.sum(dc.astype(F32), axis=0, keepdims=True)
    out_acc[...] += dot_tn(a2[...], e)
    q_acc[...] += dot_tn(n2[...], dc)
    for r in range(rows):
        im = pick[i * rows + r]
        dk_acc[im] += dk_row[r]
        dv_acc[im] += dv_row[r]

    @pl.when(i == pl.num_programs(0) - 1)
    def _():
        total = None
        for j in range(dkv.shape[0]):
            dkv[j, :, 0:width] = (dk_acc[j] * SCALE).astype(BF16)
            low = dv_acc[j].astype(BF16)
            dkv[j, :, width : 2 * width] = low
            s = jnp.sum(low.astype(F32), axis=0, keepdims=True)
            total = s if total is None else total + s
        sums_in[1:2, :] = total
        g_out[...] = out_acc[...].astype(BF16)
        fold = q_acc.shape[0] // 2
        g_q[:, 0:width] = q_acc[0:fold, :].astype(BF16)
        g_q[:, width : 2 * width] = q_acc[fold : 2 * fold, :].astype(BF16)


def kv_terms_kernel(bits, dkv, w_own, w_par, terms_own, terms_par):
    for j in range(dkv.shape[0]):
        d = dkv[j]
        terms_own[j] = dot_nt(d, w_own[...]).astype(BF16)
        terms_par[j] = dot_nt(d, w_par[...]).astype(BF16)


def kv_grad_kernel(bits, po, pp, dkv, g_out, g_q, send, keep, own_acc, par_acc, own_cols, par_cols, d_cols):
    i = pl.program_id(0)

    @pl.when(i == 0)
    def _():
        own_acc[...] = jnp.zeros_like(own_acc)
        par_acc[...] = jnp.zeros_like(par_acc)
        own_cols[...] = jnp.zeros_like(own_cols)
        par_cols[...] = jnp.zeros_like(par_cols)
        d_cols[...] = jnp.zeros_like(d_cols)

    spots = po.shape[1]
    pad = own_cols.shape[0] // po.shape[0]
    for j in range(po.shape[0]):
        at = slice(j * pad, j * pad + spots)
        own_cols[at, :] = po[j]
        par_cols[at, :] = pp[j]
        d_cols[at, :] = dkv[j]
    d = d_cols[...]
    own_acc[...] += dot_tn(own_cols[...], d)
    par_acc[...] += dot_tn(par_cols[...], d)

    @pl.when(i == pl.num_programs(0) - 1)
    def _():
        cut = g_out.shape[0]

        @pl.when(bits[0] == 0)
        def _():
            keep[0:cut, :] = g_out[...]
            keep[cut:, :] = own_acc[...].astype(BF16)
            send[0:cut, :] = g_q[...]
            send[cut:, :] = par_acc[...].astype(BF16)

        @pl.when(bits[0] != 0)
        def _():
            send[0:cut, :] = g_out[...]
            send[cut:, :] = own_acc[...].astype(BF16)
            keep[0:cut, :] = g_q[...]
            keep[cut:, :] = par_acc[...].astype(BF16)


def self_bwd_kernel(rows, length, heads, half, bits, h1, dh2, part, recv, xo, xp, gains, wo, q, k, v, p, w, a1, n1,
                    sums2, sums_in2, b_grad_a, b_grad_b,
                    dh1, part_own, part_par, send, keep, q_buf, k_buf, v_buf, out_acc, w_acc, sums, sums_in):
    i = pl.program_id(0)
    width = heads * HEAD

    @pl.when(i == 0)
    def _():
        sums[...] = jnp.zeros_like(sums)
        sums_in[...] = jnp.zeros_like(sums_in)
        out_acc[...] = jnp.zeros_like(out_acc)
        w_acc[...] = jnp.zeros_like(w_acc)

    dn = part[...].astype(F32) + recv[...].astype(F32)
    y, rs = norm_parts(h1[...])
    d = dh2[...] + norm_back(dn, y, rs, gains[1:2, :].astype(F32))
    e = d.astype(BF16)

    @pl.when(i < half)
    def _():
        dh1[...] = d
        sums[2:3, :] += jnp.sum(dn * y, axis=0, keepdims=True)
        sums[3:4, :] += jnp.sum(dn, axis=0, keepdims=True)
        sums[4:5, :] += jnp.sum(d, axis=0, keepdims=True)

    da = dot_nt(e, wo[...]).astype(BF16).astype(F32)
    qf, kf, vf = q[...].astype(F32), k[...].astype(F32), v[...].astype(F32)
    for r in range(rows):
        at = slice(r * length, (r + 1) * length)
        kr = kf[at].astype(BF16)
        vr = vf[at].astype(BF16)
        pr = p[r]
        wide_o = spread_heads(da[at], heads)
        dpt = dot_nt(vr, wide_o)
        v_buf[at, :] = dot_nn(pr, wide_o)
        pf = pr.astype(F32)
        ds = (pf * (dpt - jnp.sum(pf * dpt, axis=0, keepdims=True))).astype(BF16)
        q_buf[at, :] = join_heads(dot_tn(ds, kr), length, heads)
        k_buf[at, :] = dot_nn(ds, spread_heads(qf[at], heads))
    dqv = (q_buf[...] * SCALE).astype(BF16)
    dkv = (k_buf[...] * SCALE).astype(BF16)
    dvv = v_buf[...].astype(BF16)
    sums_in[0:1, :] += jnp.sum(dqv.astype(F32), axis=0, keepdims=True)
    sums_in[1:2, :] += jnp.sum(dvv.astype(F32), axis=0, keepdims=True)
    back = dot_nt(dqv, w[0]) + dot_nt(dkv, w[1]) + dot_nt(dvv, w[2])
    low = back.astype(BF16)

    @pl.when(i < half)
    def _():
        part_own[...] = low

    @pl.when(i >= half)
    def _():
        part_par[...] = low

    x = jnp.where(i < half, xo[...].astype(F32), xp[...].astype(F32))
    y0, _ = norm_parts(x)
    sums[0:1, :] += jnp.sum(back * y0, axis=0, keepdims=True)
    sums[1:2, :] += jnp.sum(back, axis=0, keepdims=True)
    out_acc[...] += dot_tn(a1[...], e)
    n = n1[...]
    w_acc[0] += dot_tn(n, dqv)
    w_acc[1] += dot_tn(n, dkv)
    w_acc[2] += dot_tn(n, dvv)

    @pl.when(i == pl.num_programs(0) - 1)
    def _():
        cut = out_acc.shape[0]
        fold = w_acc.shape[1] // 2
        extra = (send.shape[0] - 2 * cut)

        def folded(ref, base, j):
            ref[base : base + fold, 0:width] = w_acc[j, 0:fold, :].astype(BF16)
            ref[base : base + fold, width : 2 * width] = w_acc[j, fold : 2 * fold, :].astype(BF16)

        def first(ref):
            ref[0:cut, :] = out_acc[...].astype(BF16)
            folded(ref, cut, 0)
            pad = jnp.zeros((extra - 16, 2 * width), F32)
            ref[2 * cut :, :] = jnp.concatenate([sums[0:8, :], sums2[0:8, :], pad], axis=0).astype(BF16)

        def second(ref):
            folded(ref, 0, 1)
            folded(ref, fold, 2)
            rows_in = jnp.concatenate([sums_in[0:8, :], sums_in2[0:8, :]], axis=0)
            left = jnp.concatenate([rows_in, jnp.zeros_like(rows_in)], axis=1)
            low, high = jnp.where(bits[2] == 0, b_grad_b[...], b_grad_a[...]), jnp.where(
                bits[2] == 0, b_grad_a[...], b_grad_b[...])
            bias_rows = jnp.concatenate(
                [low, high, jnp.zeros((extra - 18, 2 * width), F32)], axis=0)
            ref[2 * fold :, :] = jnp.concatenate([left, bias_rows], axis=0).astype(BF16)

        @pl.when(bits[0] == 0)
        def _():
            first(keep)
            second(send)

        @pl.when(bits[0] != 0)
        def _():
            first(send)
            second(keep)


def text_bwd_kernel(x, dh1, part, recv, gains, out):
    dn = part[...].astype(F32) + recv[...].astype(F32)
    y, rs = norm_parts(x[...].astype(F32))
    out[...] = dh1[...] + norm_back(dn, y, rs, gains[0:1, :].astype(F32))


def widen_kernel(bits, mine, got, out):
    out[...] = jnp.where(pl.program_id(0) == bits[0], mine[...].astype(F32), got[...].astype(F32))


def open_cross_kernel(cut, bits, mine, got, g_out, g_q, g_kv):
    width = g_q.shape[1]
    zero = bits[0] == 0
    core = bits[1]
    deep = mine.shape[0] - cut
    g_out[...] = jnp.where(zero, mine[0:cut, :].astype(F32), got[0:cut, :].astype(F32))
    q = jnp.where(zero, got[0:cut, :].astype(F32), mine[0:cut, :].astype(F32))
    fold = q.shape[0]
    g_q[0:fold, :] = q[:, 0:width]
    g_q[fold : 2 * fold, :] = q[:, width : 2 * width]
    swapped = jnp.logical_xor(zero, core == 0)
    g_kv[0:deep, :] = jnp.where(swapped, got[cut:, :].astype(F32), mine[cut:, :].astype(F32))
    g_kv[deep : 2 * deep, :] = jnp.where(swapped, mine[cut:, :].astype(F32), got[cut:, :].astype(F32))


def open_self_kernel(cut, fold, bits, mine, got, g_out, g_w, rows_a, rows_in, rows_ffn):
    zero = bits[0] == 0
    width = g_w.shape[2]

    def first(at):
        return jnp.where(zero, mine[at, :].astype(F32), got[at, :].astype(F32))

    def second(at):
        return jnp.where(zero, got[at, :].astype(F32), mine[at, :].astype(F32))

    def unfold(j, v):
        g_w[j, 0:fold, :] = v[:, 0:width]
        g_w[j, fold : 2 * fold, :] = v[:, width : 2 * width]

    g_out[...] = first(slice(0, cut))
    unfold(0, first(slice(cut, cut + fold)))
    unfold(1, second(slice(0, fold)))
    unfold(2, second(slice(fold, 2 * fold)))
    r = first(slice(2 * cut, 2 * cut + 16))
    rows_a[...] = jnp.concatenate([r[0:1], r[2:3], r[8:9], r[1:2], r[3:4], r[9:10], r[4:5], r[10:12], r[0:7]], axis=0)
    r = second(slice(2 * fold, 2 * fold + 32))
    rows_in[...] = jnp.concatenate([r[0:2, 0:width], r[8:10, 0:width]], axis=0)
    rows_ffn[...] = r[16:18]


def whole(shape):
    zeros = (0,) * len(shape)
    return pl.BlockSpec(shape, lambda *_: zeros)


def call(kernel, name, grid, ins, outs, args, scratch=(), prefetch=0, flops=0, exps=0):
    moved = sum(a.size * a.dtype.itemsize for a in args) + sum(
        functools.reduce(lambda u, v: u * v, s.shape, 1) * s.dtype.itemsize for s, _ in outs
    )
    return pl.pallas_call(
        kernel,
        out_shape=[s for s, _ in outs],
        grid_spec=pltpu.PrefetchScalarGridSpec(
            num_scalar_prefetch=prefetch,
            grid=grid,
            in_specs=list(ins),
            out_specs=[b for _, b in outs],
            scratch_shapes=list(scratch),
        ),
        compiler_params=pltpu.CompilerParams(vmem_limit_bytes=VMEM_BYTES),
        cost_estimate=pl.CostEstimate(flops=flops, transcendentals=exps, bytes_accessed=moved),
        name=name,
    )(*args)


def local(n_dp, plans, text, patches, segment_ids, image_of_row, gains, shifts, self_qkv, in_bias, self_out,
          cross_q, cross_kv, cross_out, ffn_in, ffn_in_bias, ffn_out, out_bias, cotangent):
    core = lax.axis_index("tensor")
    dp = lax.axis_index("dp")
    own, width = text.shape
    tokens = 2 * own
    rows, length = segment_ids.shape
    local_width = self_out.shape[0]
    heads = local_width // HEAD
    images, spots, half_dv = patches.shape
    hidden = ffn_in.shape[1]
    wide = hidden // 2
    block_rows = rows // 2
    block = block_rows * length
    steps = tokens // block
    half = steps // 2
    sd = jax.ShapeDtypeStruct

    swap = lambda v: lax.ppermute(v, "tensor", [(0, 1), (1, 0)])
    text_par = swap(text)
    cot_par = swap(cotangent)
    patches_par = swap(patches)

    def bit_of(level):
        return jnp.where(core == 0, dp >> level[0], dp >> level[1]) & 1

    def send_along(value, level):
        perm = [(d * 2 + t, (d ^ (1 << level[t])) * 2 + t) for d in range(n_dp) for t in range(2)]
        return lax.ppermute(value, ("dp", "tensor"), perm)

    def add(a, b):
        return (a.astype(F32) + b.astype(F32)).astype(BF16)

    def after(value, *others):
        return lax.optimization_barrier((value,) + others)[0]

    def reduce_chain(send, keep, plan):
        halving, doubling = plan
        got = yield send, halving[0]
        keep = keep()
        for level in halving[1:]:
            n = keep.shape[0] // 2
            bit = bit_of(level)
            cut = lambda v, b: lax.dynamic_slice_in_dim(v, b * n, n, axis=0)
            send = add(cut(keep, 1 - bit), cut(got, 1 - bit))
            keep = add(cut(keep, bit), cut(got, bit))
            got = yield send, level
        value = add(keep, got)
        for level in doubling:
            got = yield value, level
            value = add(value, got)
        for level in reversed(halving[1:]):
            got = yield value, level
            place = lax.broadcasted_iota(jnp.int32, (2,) + value.shape, 0)
            value = jnp.where(place == bit_of(level), value[None], got[None]).reshape(-1, value.shape[1])
        got = yield value, halving[0]
        return value, got

    class Chain:
        def __init__(self, send, keep, plan):
            self.steps = reduce_chain(send, keep, plan)
            self.result = None
            self.sent, self.level = next(self.steps)

        def launch(self):
            self.got = send_along(self.sent, self.level)

        def advance(self, *hold):
            got = after(self.got, *hold) if hold else self.got
            try:
                self.sent, self.level = self.steps.send(got)
            except StopIteration as stop:
                self.result = stop.value

    def fence(chains, gate, *done):
        values = lax.optimization_barrier(tuple(c.sent for c in chains) + (gate,) + done)
        for c, v in zip(chains, values):
            c.sent = v
            c.launch()
        return values[len(chains)]

    first_bits = [
        jnp.stack([bit_of(plan[0][0]), core, bit_of(plans[0][0][0])]).astype(jnp.int32) for plan in plans]
    bits_out, bits_in, bits_cross, bits_self = first_bits

    w3 = jnp.transpose(self_qkv, (1, 0, 2))
    wkv = cross_kv.reshape(cross_kv.shape[0], 2 * local_width)
    flip = lambda v: jnp.where(core == 0, v, jnp.roll(v, rows // 2, axis=0))
    seg = flip(segment_ids)
    pick = flip(image_of_row)
    segk = seg[:, :, None]
    segq = jnp.tile(seg, (1, heads))[:, None, :]

    tok = lambda n: pl.BlockSpec((block, n), lambda i, *_: (i, 0))
    tok_other = lambda n: pl.BlockSpec((block, n), lambda i, *_: ((i + half) % steps, 0))
    tok_own = lambda n: pl.BlockSpec((block, n), lambda i, *_: (jnp.minimum(i, half - 1), 0))
    tok_par = lambda n: pl.BlockSpec((block, n), lambda i, *_: (jnp.maximum(i - half, 0), 0))
    row3 = lambda a, b: pl.BlockSpec((block_rows, a, b), lambda i, *_: (i, 0, 0))
    act = lambda n, dt=BF16: (sd((tokens, n), dt), tok(n))
    full = lambda shape, dt=BF16: (sd(shape, dt), whole(shape))
    ql = heads * length
    sizes = (block_rows, length, heads, half)

    n1, q, k, v, p1, a1, part1 = call(
        functools.partial(self_fwd_kernel, *sizes), "self_fwd", (steps,),
        [tok_own(width), tok_par(width), whole(gains.shape), whole(shifts.shape), whole(w3.shape),
         whole(in_bias.shape), whole(self_out.shape), row3(length, 1), row3(1, ql)],
        [act(width), act(local_width), act(local_width), act(local_width),
         (sd((rows, length, ql), BF16), row3(length, ql)), act(local_width), act(width)],
        (text, text_par, gains, shifts, w3, in_bias, self_out, segk, segq),
        flops=2 * tokens * width * 4 * local_width, exps=rows * length * ql)
    recv1 = swap(part1)

    kv_bias = jnp.concatenate([jnp.zeros((local_width,), F32), in_bias[3].astype(F32)])[None, :]
    place = jnp.full((1,), core, jnp.int32)
    group = 3 if images % 3 == 0 else 1
    image_block = lambda n: pl.BlockSpec((group, spots, n), lambda i, *_: (i, 0, 0))
    (kv,) = call(
        project_kernel, "project", (images // group,),
        [image_block(half_dv), image_block(half_dv),
         pl.BlockSpec((half_dv, 2 * local_width), lambda i, c: (c[0], 0)),
         pl.BlockSpec((half_dv, 2 * local_width), lambda i, c: (1 - c[0], 0)),
         whole(kv_bias.shape)],
        [(sd((images, spots, 2 * local_width), BF16), image_block(2 * local_width))],
        (place, patches, patches_par, wkv, wkv, kv_bias), prefetch=1,
        flops=4 * images * spots * 2 * half_dv * local_width)

    h1, n2, c2, p2, a2, part2 = call(
        functools.partial(cross_fwd_kernel, *sizes), "cross_fwd", (steps,),
        [tok_own(width), tok_par(width), tok(width), tok_other(width), whole(gains.shape), whole(shifts.shape),
         whole(in_bias.shape), whole(out_bias.shape), whole(cross_q.shape), whole(kv.shape), whole(cross_out.shape)],
        [act(width, F32), act(width), act(local_width), (sd((rows, spots, ql), BF16), row3(spots, ql)),
         act(local_width), act(width)],
        (pick, text, text_par, part1, recv1, gains, shifts, in_bias, out_bias, cross_q, kv, cross_out), prefetch=1,
        flops=2 * tokens * width * 2 * local_width + 4 * rows * ql * spots * local_width, exps=rows * ql * spots)
    recv2 = swap(part2)

    own_spec = lambda n: (sd((own, n), BF16), tok_own(n))
    par_spec = lambda n: (sd((own, n), BF16), tok_par(n))
    b_in = ffn_in_bias[None, :]
    half_specs = lambda at: [
        pl.BlockSpec((width, wide), lambda i, b: (0, at(b[0]))),
        pl.BlockSpec((1, wide), lambda i, b: (0, at(b[0]))),
        pl.BlockSpec((wide, width), lambda i, b: (at(b[0]), 0))]
    ffn_acc = [pltpu.VMEM((wide, width), F32)]
    ffn_cost = dict(flops=5 * tokens * width * hidden, exps=tokens * hidden)
    h2, n3, e3, du_a, o_sum, g_sum, out_send, b_grad_a = call(
        functools.partial(ffn_send_kernel, half), "ffn_send", (steps,),
        [tok(width), tok(width), tok_other(width), tok_own(width), tok_par(width), whole(gains.shape),
         whole(shifts.shape), whole(out_bias.shape)] + half_specs(lambda b: 1 - b),
        [act(width, F32), act(width), act(width), act(wide), act(width), act(width), full((wide, width)),
         full((1, wide), F32)],
        (bits_out, h1, part2, recv2, cotangent, cot_par, gains, shifts, out_bias, ffn_in, b_in, ffn_out),
        scratch=ffn_acc, prefetch=1, **ffn_cost)
    chain_out = Chain(out_send, lambda: out_keep, plans[0])
    gate = fence([chain_out], bits_out)
    du_b, part3_own, part3_par, pdn3, out_keep, b_grad_b = call(
        functools.partial(ffn_keep_kernel, half), "ffn_keep", (steps,),
        [tok(width), tok(width), tok(width), tok(width)] + half_specs(lambda b: b),
        [act(wide), own_spec(width), par_spec(width), act(width), full((wide, width)), full((1, wide), F32)],
        (gate, n3, e3, o_sum, g_sum, ffn_in, b_in, ffn_out),
        scratch=ffn_acc, prefetch=1, **ffn_cost)
    recv3 = swap(pdn3)
    chain_out.advance()
    recv_out = swap(part3_par)
    layer_out = h2[:own] + (part3_own.astype(F32) + recv_out.astype(F32)) + out_bias[2].astype(F32)

    hw = width // 2
    gate = fence([chain_out], jnp.stack([bits_out[0], bits_in[0]]), pdn3)
    in_send, in_keep = call(
        ffn_in_kernel, "ffn_in_grad", (2, 2),
        [pl.BlockSpec((tokens, hw), lambda j, c, b: (0, jnp.where(j == 0, 1 - b[1], b[1]))),
         whole((tokens, wide)), whole((tokens, wide))],
        [(sd((width, wide), BF16), pl.BlockSpec((hw, wide), lambda j, c, b: (jnp.where(j == 0, c, 1), 0))),
         (sd((width, wide), BF16), pl.BlockSpec((hw, wide), lambda j, c, b: (jnp.where(j == 0, 0, c), 0)))],
        (gate, n3, du_a, du_b), prefetch=1, flops=2 * tokens * width * hidden)

    chain_in = Chain(in_send, lambda: in_keep, plans[1])
    chain_out.advance()
    gate = fence([chain_out, chain_in], pick)
    dh2, dkv, pdn2, sums2, sums_in2, g_cross_out, g_cross_q = call(
        functools.partial(cross_bwd_kernel, *sizes), "cross_bwd", (steps,),
        [tok(width), tok(width), tok_other(width), tok_own(width), tok_par(width), whole(gains.shape),
         whole(cross_out.shape), tok(local_width), row3(spots, ql), whole(kv.shape), whole(cross_q.shape),
         tok(local_width), tok(width)],
        [act(width, F32), full(kv.shape), act(width), full((8, width), F32), full((8, local_width), F32),
         full((local_width, width)), full((hw, width))],
        (gate, h2, pdn3, recv3, cotangent, cot_par, gains, cross_out, c2, p2, kv, cross_q, a2, n2), prefetch=1,
        scratch=[pltpu.VMEM((images, spots, local_width), F32)] * 2
        + [pltpu.VMEM((block_rows, spots, local_width), F32)] * 2
        + [pltpu.VMEM((block, local_width), F32), pltpu.VMEM((local_width, width), F32),
           pltpu.VMEM((width, local_width), F32)],
        flops=2 * tokens * width * 4 * local_width + 8 * rows * ql * spots * local_width)
    recv_dn2 = swap(pdn2)
    chain_out.advance()
    chain_in.advance()
    gate = fence([chain_out, chain_in], bits_cross, pdn2)

    deep = local_width + half_dv
    slots = -(-spots // 16) * 16
    cross_send, cross_keep = call(
        kv_grad_kernel, "kv_grad", (images // group,),
        [image_block(half_dv), image_block(half_dv), image_block(2 * local_width), whole(g_cross_out.shape),
         whole(g_cross_q.shape)],
        [full((deep, width)), full((deep, width))],
        (gate, patches, patches_par, dkv, g_cross_out, g_cross_q), prefetch=1,
        scratch=[pltpu.VMEM((half_dv, width), F32)] * 2
        + [pltpu.VMEM((group * slots, half_dv), BF16)] * 2 + [pltpu.VMEM((group * slots, 2 * local_width), BF16)],
        flops=4 * images * spots * 2 * half_dv * local_width)
    chain_cross = Chain(cross_send, lambda: cross_keep, plans[2])
    chain_out.advance()
    chain_in.advance()
    gate = fence([chain_out, chain_in, chain_cross], bits_self)

    extra = 32
    tall = 2 * local_width + extra
    dh1, part1_own, part1_par, self_send, self_keep = call(
        functools.partial(self_bwd_kernel, *sizes), "self_bwd", (steps,),
        [tok(width), tok(width), tok(width), tok_other(width), tok_own(width), tok_par(width), whole(gains.shape),
         whole(self_out.shape), tok(local_width), tok(local_width), tok(local_width), row3(length, ql),
         whole(w3.shape), tok(local_width), tok(width), whole((8, width)), whole((8, local_width)),
         whole((1, wide)), whole((1, wide))],
        [(sd((own, width), F32), tok_own(width)), own_spec(width), par_spec(width), full((tall, width)),
         full((tall, width))],
        (gate, h1, dh2, pdn2, recv_dn2, text, text_par, gains, self_out, q, k, v, p1, w3, a1, n1, sums2,
         sums_in2, b_grad_a, b_grad_b), prefetch=1,
        scratch=[pltpu.VMEM((block, local_width), F32)] * 3
        + [pltpu.VMEM((local_width, width), F32), pltpu.VMEM((3, width, local_width), F32),
           pltpu.VMEM((8, width), F32), pltpu.VMEM((8, local_width), F32)],
        flops=2 * tokens * width * 8 * local_width)
    recv_dn1 = swap(part1_par)
    chain_self = Chain(self_send, lambda: self_keep, plans[3])
    chain_out.advance()
    chain_in.advance()
    chain_cross.advance()
    last = fence([chain_cross, chain_in, chain_out, chain_self], part1_own)
    terms_own, terms_par = call(
        kv_terms_kernel, "kv_terms", (images // group,),
        [image_block(2 * local_width), pl.BlockSpec((half_dv, 2 * local_width), lambda i, c: (c[1], 0)),
         pl.BlockSpec((half_dv, 2 * local_width), lambda i, c: (1 - c[1], 0))],
        [(sd(patches.shape, BF16), image_block(half_dv)), (sd(patches.shape, BF16), image_block(half_dv))],
        (after(bits_cross, part1_own), dkv, wkv, wkv), prefetch=1,
        flops=4 * images * spots * 2 * half_dv * local_width)
    patch_grad = terms_own.astype(F32) + swap(terms_par).astype(F32)
    text_block = own // 2
    half_block = pl.BlockSpec((text_block, width), lambda i, *_: (i, 0))
    (text_grad,) = call(
        text_bwd_kernel, "text_bwd", (2,),
        [half_block, half_block, half_block, half_block, whole(gains.shape)],
        [(sd((own, width), F32), half_block)],
        (text, dh1, part1_own, recv_dn1, gains))

    piece = pl.BlockSpec((hw, width), lambda j, c, b: (c, 0))
    open_cross = lambda r: (r[2].reshape(cross_kv.shape), r[0], r[1])
    opens = {
        chain_out: lambda got: call(
            widen_kernel, "open_ffn_out", (2, wide // hw), [piece, piece],
            [(sd((hidden, width), F32), pl.BlockSpec((hw, width), lambda j, c, b: (j * (wide // hw) + c, 0)))],
            (bits_out,) + got, prefetch=1),
        chain_in: lambda got: call(
            widen_kernel, "open_ffn_in", (2, 2), [piece, piece],
            [(sd((width, hidden), F32), pl.BlockSpec((hw, wide), lambda j, c, b: (j, c)))],
            (bits_in,) + got, prefetch=1),
        chain_cross: lambda got: open_cross(call(
            functools.partial(open_cross_kernel, local_width), "open_cross", (1,),
            [whole((deep, width)), whole((deep, width))],
            [full((local_width, width), F32), full((width, local_width), F32), full((2 * half_dv, width), F32)],
            (bits_cross,) + got, prefetch=1)),
        chain_self: lambda got: call(
            functools.partial(open_self_kernel, local_width, hw), "open_self", (1,),
            [whole((tall, width)), whole((tall, width))],
            [full((local_width, width), F32), full((3, width, local_width), F32), full((16, width), F32),
             full((4, local_width), F32), full((2, wide), F32)],
            (bits_self,) + got, prefetch=1),
    }
    o, i, c, s = chain_out, chain_in, chain_cross, chain_self
    opened, filler = {}, (terms_own,)
    order = [c, i, c, s, i, s, o, c, i, s, c, s, c, s, o, s, c, s, i]
    while len(opened) < len(opens):
        chain = order.pop(0) if order else next(v for v in opens if v not in opened)
        if chain in opened:
            continue
        chain.advance(last, *filler)
        filler = ()
        if chain.result is None:
            chain.launch()
            last = chain.sent
        else:
            opened[chain] = opens[chain](chain.result)
            last = opened[chain][0]
    (ffn_out_grad,), (ffn_in_grad,) = opened[o], opened[i]
    cross_kv_grad, cross_out_grad, cross_q_grad = opened[c]
    self_out_grad, qkv_grad, rows_a, in_bias_grad, rows_ffn = opened[s]
    self_qkv_grad = jnp.transpose(qkv_grad, (1, 0, 2))

    rows_a = rows_a + swap(rows_a)
    gains_grad, shifts_grad, out_bias_grad = rows_a[0:3], rows_a[3:6], rows_a[6:9]
    ffn_in_bias_grad = rows_ffn.reshape(hidden)

    return (layer_out, text_grad, patch_grad, gains_grad, shifts_grad, self_qkv_grad, in_bias_grad, self_out_grad,
            cross_q_grad, cross_kv_grad, cross_out_grad, ffn_in_grad, ffn_in_bias_grad, ffn_out_grad, out_bias_grad)


def make_plans(mesh):
    bits = mesh.shape["dp"].bit_length() - 1
    third = (bits + 1) // 4
    x, y, z = list(range(third)), list(range(third, 2 * third)), list(range(2 * third, bits))
    flat = list(zip(x + y, y + x))
    up = list(zip(z, z))
    return [(flat + up[:1], up[1:])] * 4


def solution(mesh):
    both = P(("dp", "tensor"), None)
    in_specs = (both, P("dp", None, "tensor"), P("dp", None), P("dp"), P(), P(), P(None, None, "tensor"),
                P(None, "tensor"), P("tensor", None), P(None, "tensor"), P(None, None, "tensor"), P("tensor", None),
                P(None, "tensor"), P("tensor"), P("tensor", None), P(), both)
    out_specs = (both, both, P("dp", None, "tensor"), P(), P(), P(None, None, "tensor"), P(None, "tensor"),
                 P("tensor", None), P(None, "tensor"), P(None, None, "tensor"), P("tensor", None), P(None, "tensor"),
                 P("tensor"), P("tensor", None), P())
    fn = functools.partial(local, mesh.shape["dp"], make_plans(mesh))
    return jax.shard_map(fn, mesh=mesh, in_specs=in_specs, out_specs=out_specs, check_vma=False)
```
